256 devices in a mesh: group: 2 (over core), dp: 16 (over x, z_hi), mp: 8 (over y, z_lo).
Axes of the slice: x: 4, y: 4, z: 8 (z_hi: 4, z_lo: 2; z = z_hi * 2 + z_lo), core: 2. Of those that a mesh axis runs over, the one named last changes fastest.
Arguments:
- noise_seeds: int32 [32], P(('group', 'dp')), may hold values from 0 to 16777215
- timestep_ids: int32 [32], P(('group', 'dp')), may hold values from 0 to 999
- gen_up: bfloat16 [3072, 6144], P(('group', 'dp'), 'mp'), may hold values from -0.109375 to 0.109375
- gen_down: bfloat16 [6144, 3072], P('mp', ('group', 'dp')), may hold values from -0.08930431 to 0.08930431
- score_qkv: bfloat16 [2, 3, 3072, 3072], P('group', None, None, 'mp'), may hold values from -0.109375 to 0.109375
- score_out: bfloat16 [2, 3072, 3072], P('group', 'mp'), may hold values from -0.109375 to 0.109375
Outputs:
- latents: bfloat16 [32, 256, 3072], P(('group', 'dp'), None, 'mp')
- score_gap: bfloat16 [32, 256, 3072], P(('group', 'dp'), None, 'mp')
- grad_up: bfloat16 [3072, 6144], P(('group', 'dp'), 'mp')
- grad_down: bfloat16 [6144, 3072], P('mp', ('group', 'dp'))
The draws below stay inside these ranges and needn't reach their ends.
All inputs are finite; a program needn't handle non-finite values.
Results may differ from the reference program's by a relative error of at most 0.03.
Values may be sent and summed in bfloat16 or wider, within the bound.
No kernel may reach another device: no remote copies, remote signals or barrier semaphores. Data moves between devices by JAX's collectives and lax.ppermute only.
A program may use at most 128 MiB of HBM per device.

```python
import jax
import jax.numpy as jnp
from jax import lax

D = 3072
HEADS = 24
HEAD_DIM = 128
FF = 6144
SEQ = 256
STEPS = 1000
BATCH = 32
N_MP = 8


def draw_gen_down(key, part):
    scale = FF ** (-0.5)
    base = jnp.clip(jax.random.normal(key, (FF, D), jnp.float32), -6.0, 6.0)
    centred = base - jnp.mean(base, axis=0, keepdims=True)
    return (centred * scale).astype(jnp.bfloat16)


def place_ends(result, stream_key, low, largest):
    place = [jax.random.randint(jax.random.fold_in(stream_key, axis), (), 0, length) for axis, length in enumerate(result.shape)]
    longest = result.shape.index(max(result.shape))
    neighbour = place[:longest] + [(place[longest] + 1) % result.shape[longest]] + place[longest + 1:]
    return result.at[tuple(place)].set(low).at[tuple(neighbour)].set(largest)


def levels(rng, shape, pieces, low, high):
    level, own = 1.0, jax.random.fold_in(rng, 6)
    for axis_at, shards_of in pieces:
        steps = jnp.exp(jax.random.uniform(jax.random.fold_in(own, axis_at), (shards_of,), jnp.float32, low / len(pieces), high / len(pieces)))
        level = level * jnp.repeat(steps, shape[axis_at] // shards_of).reshape([-1 if axis == axis_at else 1 for axis in range(len(shape))])
    return level


def bell_draw(key, shape, deviation, most, pieces=(), kind=jnp.bfloat16):
    array = deviation * jax.random.normal(key, shape, jnp.float32)
    if pieces:
        array = array * levels(key, shape, pieces, -0.22, 0.18)
    return jnp.clip(array, -most, most).astype(kind)


def setup_inputs(seed: int = 0) -> dict:
    arg_keys = jax.random.split(jax.random.key(seed), 7)
    noise_seeds = place_ends(jax.random.randint(arg_keys[0], (BATCH,), 0, 16777216), jax.random.fold_in(arg_keys[0], 1), 0, 16777215).astype(jnp.int32)
    timestep_ids = place_ends(jax.random.randint(arg_keys[1], (BATCH,), 0, STEPS), jax.random.fold_in(arg_keys[1], 1), 0, STEPS - 1).astype(jnp.int32)
    gen_up = bell_draw(arg_keys[2], (D, FF), D ** -0.5, 0.109375, ((0, 32), (1, 8)))
    gen_down = draw_gen_down(jax.random.fold_in(arg_keys[6], 71), 0)
    score_qkv = bell_draw(arg_keys[4], (2, 3, D, D), D ** -0.5, 0.109375, ((0, 2), (3, 8)))
    score_out = bell_draw(arg_keys[5], (2, D, D), D ** -0.5, 0.109375, ((0, 2), (1, 8)))
    return dict(noise_seeds=noise_seeds, timestep_ids=timestep_ids, gen_up=gen_up, gen_down=gen_down, score_qkv=score_qkv, score_out=score_out)


NORM_EPS = 1e-06
ROOT_THREE = 1.7320508
GELU_SCALE = 0.7978845608

def hashed(seed_grid, stream, feat_start, feat_count, length):
    shape = (1, length, feat_count)
    tokens = lax.broadcasted_iota(jnp.int32, shape, 1)
    feature = lax.broadcasted_iota(jnp.int32, shape, 2) + feat_start
    mixing = seed_grid * 747796405 + stream * 374761393 + tokens * 1103515245 + feature * 668265263
    mixing = mixing ^ mixing >> 15
    mixing = mixing * 1274126177
    mixing = mixing ^ mixing >> 13
    mixing = mixing * 1911520717
    mixing = mixing ^ mixing >> 16
    level = (mixing >> 7 & 65535).astype(jnp.float32)
    return ((level + 0.5) * (2.0 / 65536.0) - 1.0) * ROOT_THREE

def rms_norm(value):
    return value * lax.rsqrt(lax.optimization_barrier(jnp.mean(value * value, axis=-1, keepdims=True)) + NORM_EPS)

def gelu_slope(value):
    inner = GELU_SCALE * (value + 0.044715 * value * value * value)
    bend = jnp.tanh(inner)
    return 0.5 * (1.0 + bend) + 0.5 * value * (1.0 - bend * bend) * GELU_SCALE * (1.0 + 3.0 * 0.044715 * value * value)

def rounded(value):
    return lax.optimization_barrier(value.astype(jnp.bfloat16)).astype(jnp.float32)

def block_sum(left, right, blocks):
    size = left.shape[1] // blocks
    total = jnp.zeros((left.shape[0], right.shape[1]), jnp.float32)
    for block in range(blocks):
        term = jnp.dot(left[:, block * size:(block + 1) * size], right[block * size:(block + 1) * size], preferred_element_type=jnp.float32)
        total = total + rounded(term)
    return total

def score_net(noisy, weights_in, weights_out):
    normed = rms_norm(noisy.astype(jnp.float32)).astype(jnp.bfloat16).reshape(BATCH * SEQ, D)
    shape = (BATCH, SEQ, HEADS, HEAD_DIM)
    query = jnp.dot(normed, weights_in[0], preferred_element_type=jnp.float32).astype(jnp.bfloat16).reshape(shape)
    keys = jnp.dot(normed, weights_in[1], preferred_element_type=jnp.float32).astype(jnp.bfloat16).reshape(shape)
    values = jnp.dot(normed, weights_in[2], preferred_element_type=jnp.float32).astype(jnp.bfloat16).reshape(shape)

    def attend(triple):
        asked, keyed, valued = triple
        scores = jnp.einsum('qhe,khe->hqk', asked.astype(jnp.float32), keyed.astype(jnp.float32)) * HEAD_DIM ** (-0.5)
        expo = jnp.exp(scores)
        probs = (expo / lax.optimization_barrier(jnp.sum(expo, axis=-1, keepdims=True))).astype(jnp.bfloat16)
        return jnp.einsum('hqk,khe->qhe', probs.astype(jnp.float32), valued.astype(jnp.float32)).astype(jnp.bfloat16)
    attended = lax.map(attend, (query, keys, values)).reshape(BATCH * SEQ, D)
    return block_sum(attended, weights_out, N_MP).astype(jnp.bfloat16).reshape(BATCH, SEQ, D)

def reference(noise_seeds, timestep_ids, gen_up, gen_down, score_qkv, score_out):
    seed_grid = noise_seeds[:, None, None]
    start_noise = hashed(seed_grid, 0, 0, D, SEQ)
    normed = rms_norm(start_noise).astype(jnp.bfloat16).reshape(BATCH * SEQ, D)
    before = jnp.dot(normed, gen_up, preferred_element_type=jnp.float32)
    hidden = jax.nn.gelu(before, approximate=True).astype(jnp.bfloat16)
    mixed = block_sum(hidden, gen_down, N_MP)
    latents = (start_noise + mixed.reshape(BATCH, SEQ, D)).astype(jnp.bfloat16)
    shift = ((timestep_ids.astype(jnp.float32) + 0.5) / STEPS)[:, None, None]
    fresh = hashed(seed_grid, 1, 0, D, SEQ)
    noisy = ((1.0 - shift) * latents.astype(jnp.float32) + shift * fresh).astype(jnp.bfloat16)
    real_pred = score_net(noisy, score_qkv[0], score_out[0])
    fake_pred = score_net(noisy, score_qkv[1], score_out[1])
    score_gap = (fake_pred.astype(jnp.float32) - real_pred.astype(jnp.float32)).astype(jnp.bfloat16)

    def accumulate(carry, items):
        grad_u, grad_d = carry
        hid, nrm, bef, gapped = items
        down_term = jnp.dot(hid.T, gapped, preferred_element_type=jnp.float32) / BATCH
        slope = jnp.dot(gapped, gen_down.T, preferred_element_type=jnp.float32)
        change = (slope * gelu_slope(bef)).astype(jnp.bfloat16)
        up_term = jnp.dot(nrm.T, change, preferred_element_type=jnp.float32) / BATCH
        return ((grad_u + rounded(up_term), grad_d + rounded(down_term)), None)
    start = (jnp.zeros((D, FF), jnp.float32), jnp.zeros((FF, D), jnp.float32))
    items = (hidden.reshape(BATCH, SEQ, FF), normed.reshape(BATCH, SEQ, D), before.reshape(BATCH, SEQ, FF), score_gap)
    (grad_u, grad_d), unused = lax.scan(accumulate, start, items)
    return (latents, score_gap, grad_u.astype(jnp.bfloat16), grad_d.astype(jnp.bfloat16))
```

```python
import jax
import jax.numpy as jnp
from jax import lax
from jax.sharding import Mesh
from jax.sharding import PartitionSpec as P

D = 3072
FF_LOCAL = 768
HEAD_DIM = 128
SEQ = 256
STEPS = 1000
BATCH = 32
SHARD = 96
BLOCK = 384
SAMPLES = ("group", "x", "zh")
MODEL = ("y", "zl")

NORM_EPS = 1e-06
ROOT_THREE = 1.7320508
GELU_SCALE = 0.7978845608


def hop(value, axis, step):
    n = lax.axis_size(axis)
    return lax.ppermute(value, axis, [(i, (i + step) % n) for i in range(n)])


def wide(value):
    return value.astype(jnp.float32)


def narrow(value):
    return value.astype(jnp.bfloat16)


def ring_gather(block, axis):
    half = block.shape[0] // 2
    top, bottom = block[:half], block[half:]
    left_top = hop(top, axis, 1)
    right_bottom = hop(bottom, axis, -1)
    left_bottom = hop(bottom, axis, 1)
    right_top = hop(top, axis, -1)
    far_top = hop(left_top, axis, 1)
    far_bottom = hop(right_bottom, axis, -1)
    return [
        block,
        jnp.concatenate([right_top, right_bottom]),
        jnp.concatenate([far_top, far_bottom]),
        jnp.concatenate([left_top, left_bottom]),
    ]


def ring_scatter(parts, axis):
    own, right, far, left = parts
    half = own.shape[0] // 2
    for_right = hop(far[:half], axis, 1)
    for_left = hop(far[half:], axis, -1)
    from_left_bottom = hop(right[half:], axis, 1)
    from_right_top = hop(left[:half], axis, -1)
    from_left_top = hop(narrow(wide(right[:half]) + wide(for_right)), axis, 1)
    from_right_bottom = hop(narrow(wide(left[half:]) + wide(for_left)), axis, -1)
    top = wide(own[:half]) + wide(from_right_top) + wide(from_left_top)
    bottom = wide(own[half:]) + wide(from_left_bottom) + wide(from_right_bottom)
    return jnp.concatenate([top, bottom])


def model_gather(block):
    other = hop(block, "zl", 1)
    return jnp.stack(ring_gather(block, "y") + ring_gather(other, "y"))


def model_scatter(part):
    other = ring_scatter([part(dy, 1) for dy in range(4)], "y")
    crossed = hop(narrow(other), "zl", 1)
    own = ring_scatter([part(dy, 0) for dy in range(4)], "y")
    return own + wide(crossed)


def pick(stack, index):
    return lax.dynamic_index_in_dim(stack, index, 0, keepdims=False)


def hashed(seed, stream, feature, length):
    tokens = lax.broadcasted_iota(jnp.int32, (length, feature.shape[0]), 0)
    mixing = (
        seed * 747796405
        + stream * 374761393
        + tokens * 1103515245
        + feature[None, :] * 668265263
    )
    mixing = mixing ^ mixing >> 15
    mixing = mixing * 1274126177
    mixing = mixing ^ mixing >> 13
    mixing = mixing * 1911520717
    mixing = mixing ^ mixing >> 16
    level = (mixing >> 7 & 65535).astype(jnp.float32)
    return ((level + 0.5) * (2.0 / 65536.0) - 1.0) * ROOT_THREE


def rms_norm(value):
    return value * lax.rsqrt(jnp.mean(value * value, axis=-1, keepdims=True) + NORM_EPS)


def gelu_slope(value):
    inner = GELU_SCALE * (value + 0.044715 * value * value * value)
    bend = jnp.tanh(inner)
    return 0.5 * (1.0 + bend) + 0.5 * value * (1.0 - bend * bend) * GELU_SCALE * (
        1.0 + 3.0 * 0.044715 * value * value
    )


def dot(left, right, left_dim=1, right_dim=0):
    return lax.dot_general(
        left, right, (((left_dim,), (right_dim,)), ((), ())), preferred_element_type=jnp.float32
    )


def attend(normed, weights_in):
    heads = BLOCK // HEAD_DIM
    query, keys, values = (
        narrow(dot(normed, weights_in[k])).reshape(SEQ, heads, HEAD_DIM) for k in range(3)
    )
    scores = jnp.einsum(
        "qhe,khe->hqk", query, keys, preferred_element_type=jnp.float32
    ) * HEAD_DIM ** (-0.5)
    expo = jnp.exp(scores)
    probs = narrow(expo / jnp.sum(expo, axis=-1, keepdims=True))
    attended = jnp.einsum("hqk,khe->qhe", probs, values, preferred_element_type=jnp.float32)
    return narrow(attended).reshape(SEQ, BLOCK)


def per_device(noise_seeds, timestep_ids, gen_up, gen_down, score_qkv, score_out):
    group, x, zh = (lax.axis_index(a) for a in SAMPLES)
    y, zl = (lax.axis_index(a) for a in MODEL)
    seed = noise_seeds[0]

    up_z = ring_gather(gen_up, "zh")
    up_near = ring_gather(gen_up, "x")
    down_z = ring_gather(gen_down.T, "zh")
    up_rest = ring_gather(jnp.concatenate(up_z[1:]), "x")
    up_own = [jnp.concatenate([a, b]) for a, b in zip(up_near, up_rest)]
    up_other = [hop(block, "group", 1) for block in up_own]
    down_block = lax.dynamic_slice_in_dim(
        jnp.concatenate(down_z + down_z[:3]), ((4 - zh) & 3) * SHARD, BLOCK, 0
    )
    down_own = ring_gather(down_block, "x")
    down_other = [hop(block, "group", 1) for block in down_own]
    qkv_own, out_own = score_qkv[0], score_out[0]
    qkv_other = hop(qkv_own, "group", 1)
    out_other = hop(out_own, "group", 1)

    index = lax.iota(jnp.int32, D)
    feature = (
        ((((index // 1536) ^ group) * 4 + ((index // BLOCK + x) & 3)) * 4
        + ((index // SHARD + zh) & 3)) * SHARD
        + index % SHARD
    )
    normed = lax.optimization_barrier(narrow(rms_norm(hashed(seed, 0, feature, SEQ))))
    normed_crossed = hop(normed[:, 1536:], "group", 1)
    normed_pair = jnp.concatenate([normed[:, :1536], normed_crossed])
    before = sum(
        dot(normed[:, k * BLOCK : (k + 1) * BLOCK], block)
        for k, block in enumerate(up_own + up_other)
    )
    hidden = narrow(jax.nn.gelu(before, approximate=True))
    hidden_pair = jnp.concatenate([hidden, hop(hidden, "group", 1)])

    down_all = down_own + down_other
    partial = jnp.stack([narrow(dot(hidden, block, 1, 1)) for block in down_all])

    def generator_part(dy, dz):
        owner = ((y + dy) & 3) * 2 + (zl ^ dz)
        return pick(partial, ((owner >> 2) ^ group) * 4 + ((owner - x) & 3))

    mixed = model_scatter(generator_part)
    local = lax.iota(jnp.int32, BLOCK) + (y * 2 + zl) * BLOCK
    shift = (timestep_ids[0].astype(jnp.float32) + 0.5) / STEPS
    latent = narrow(hashed(seed, 0, local, SEQ) + mixed)
    fresh = hashed(seed, 1, local, SEQ)
    noisy = narrow((1.0 - shift) * wide(latent) + shift * fresh)

    def place(j):
        return ((j & 1) ^ zl) * 4 + (((j >> 1) - y) & 3)

    noisy_all = model_gather(noisy)
    noisy_full = jnp.concatenate([pick(noisy_all, place(j)) for j in range(8)], axis=1)
    score_normed = lax.optimization_barrier(narrow(rms_norm(wide(noisy_full))))
    sign = wide(2 * group - 1)
    attended_own = narrow(wide(attend(score_normed, qkv_own)) * sign)
    attended_other = narrow(wide(attend(score_normed, qkv_other)) * -sign)
    gap_partial = narrow(dot(attended_own, out_own) + dot(attended_other, out_other))
    gap_parts = jnp.moveaxis(gap_partial.reshape(SEQ, 8, BLOCK), 1, 0)

    def gap_part(dy, dz):
        return pick(gap_parts, ((y + dy) & 3) * 2 + (zl ^ dz))

    gap = narrow(model_scatter(gap_part))

    gap_all = model_gather(gap)
    gap_abs = jnp.stack([pick(gap_all, place(j)) for j in range(8)])
    crossed = hop(lax.dynamic_slice_in_dim(gap_abs, (1 - group) * 4, 4, 0), "group", 1)
    kept = lax.dynamic_slice_in_dim(gap_abs, group * 4, 4, 0)
    gap_pair = jnp.concatenate([kept, crossed], axis=1)
    down_grads = [
        narrow(dot(pick(gap_pair, (x + dx) & 3), hidden_pair, 0, 0) / BATCH) for dx in range(4)
    ]
    down_sum = narrow(ring_scatter(down_grads, "x")).reshape(4, SHARD, FF_LOCAL)
    grad_down = narrow(ring_scatter([pick(down_sum, (zh + dz) & 3) for dz in range(4)], "zh")).T

    slope = sum(
        dot(pick(gap_abs, (group ^ (k // 4)) * 4 + ((x + k) & 3)), block)
        for k, block in enumerate(down_all)
    )
    change = narrow(slope * gelu_slope(before))
    change_pair = jnp.concatenate([change, hop(change, "group", 1)])
    up_grads = [
        narrow(dot(normed_pair[:, dx * BLOCK : (dx + 1) * BLOCK], change_pair, 0, 0) / BATCH)
        for dx in range(4)
    ]
    up_sum = narrow(ring_scatter(up_grads, "x")).reshape(4, SHARD, FF_LOCAL)
    grad_up = narrow(ring_scatter([up_sum[dz] for dz in range(4)], "zh"))
    return (latent[None], gap[None], grad_up, grad_down)


def solution(mesh):
    split = Mesh(
        mesh.devices.reshape(mesh.shape["group"], 4, 4, 4, 2), ("group", "x", "zh", "y", "zl")
    )
    in_specs = (
        P(SAMPLES),
        P(SAMPLES),
        P(SAMPLES, MODEL),
        P(MODEL, SAMPLES),
        P("group", None, None, MODEL),
        P("group", MODEL, None),
    )
    out_specs = (
        P(SAMPLES, None, MODEL),
        P(SAMPLES, None, MODEL),
        P(SAMPLES, MODEL),
        P(MODEL, SAMPLES),
    )
    return jax.shard_map(
        per_device, mesh=split, in_specs=in_specs, out_specs=out_specs, check_vma=False
    )
```

```python
import jax
import jax.numpy as jnp
from jax import lax
from jax.experimental import pallas as pl
from jax.experimental.pallas import tpu as pltpu
from jax.sharding import Mesh
from jax.sharding import PartitionSpec as P

D = 3072
FF_LOCAL = 768
HEAD_DIM = 128
SEQ = 256
STEPS = 1000
BATCH = 32
SHARD = 96
BLOCK = 384
SAMPLES = ("group", "x", "zh")
MODEL = ("y", "zl")

NORM_EPS = 1e-06
ROOT_THREE = 1.7320508
GELU_SCALE = 0.7978845608


def hop(value, axis, step):
    n = lax.axis_size(axis)
    return lax.ppermute(value, axis, [(i, (i + step) % n) for i in range(n)])


def wide(value):
    return value.astype(jnp.float32)


def narrow(value):
    return value.astype(jnp.bfloat16)


def direct_gather(block, axis):
    return [block] + [hop(block, axis, -k) for k in (1, 2, 3)]


def ring_gather(block, axis):
    half = block.shape[0] // 2
    left = hop(block, axis, 1)
    right = hop(block, axis, -1)
    far_top = hop(left[:half], axis, 1)
    far_bottom = hop(right[half:], axis, -1)
    return [block, right, jnp.concatenate([far_top, far_bottom]), left]


def direct_scatter(parts, axis):
    return wide(parts[0]) + sum(wide(hop(parts[k], axis, k)) for k in (1, 3, 2))


def ring_scatter(parts, axis):
    own, right, far, left = parts
    half = own.shape[0] // 2
    for_right = hop(far[:half], axis, 1)
    for_left = hop(far[half:], axis, -1)
    right = jnp.concatenate([narrow(wide(right[:half]) + wide(for_right)), right[half:]])
    left = jnp.concatenate([left[:half], narrow(wide(left[half:]) + wide(for_left))])
    from_left = hop(right, axis, 1)
    from_right = hop(left, axis, -1)
    return wide(own) + wide(from_left) + wide(from_right)


def model_gather(block):
    return lax.all_to_all(
        jnp.broadcast_to(block[None], (8, *block.shape)), MODEL, 0, 0, tiled=True
    )


def model_scatter(parts):
    return wide(lax.all_to_all(parts, MODEL, 0, 0, tiled=True)).sum(axis=0)


def pick(stack, index):
    return lax.dynamic_index_in_dim(stack, index, 0, keepdims=False)


def hashed(seed, stream, feature, length):
    tokens = lax.broadcasted_iota(jnp.int32, (length, feature.shape[0]), 0)
    mixing = (
        seed * 747796405
        + stream * 374761393
        + tokens * 1103515245
        + feature[None, :] * 668265263
    )
    mixing = mixing ^ mixing >> 15
    mixing = mixing * 1274126177
    mixing = mixing ^ mixing >> 13
    mixing = mixing * 1911520717
    mixing = mixing ^ mixing >> 16
    level = (mixing >> 7 & 65535).astype(jnp.float32)
    return ((level + 0.5) * (2.0 / 65536.0) - 1.0) * ROOT_THREE


def rms_norm(value):
    return value * lax.rsqrt(jnp.mean(value * value, axis=-1, keepdims=True) + NORM_EPS)


def gelu_slope(value):
    inner = GELU_SCALE * (value + 0.044715 * value * value * value)
    bend = jnp.tanh(inner)
    return 0.5 * (1.0 + bend) + 0.5 * value * (1.0 - bend * bend) * GELU_SCALE * (
        1.0 + 3.0 * 0.044715 * value * value
    )


def dot(left, right, left_dim=1, right_dim=0):
    return lax.dot_general(
        left, right, (((left_dim,), (right_dim,)), ((), ())), preferred_element_type=jnp.float32
    )


def score_kernel(
    sign_ref, noisy_ref, own_ref, other_ref, out_own_ref, out_other_ref, gap_ref,
    normed_ref, qkv_ref, total_ref, mix_ref,
):
    net, step = pl.program_id(0), pl.program_id(1)

    @pl.when((net == 0) & (step == 0))
    def _():
        def square(j, total):
            block = wide(noisy_ref[j])
            return total + jnp.sum(block * block, axis=-1, keepdims=True)

        total = lax.fori_loop(0, 8, square, jnp.zeros((SEQ, 1), jnp.float32))
        scale = lax.rsqrt(total * (1.0 / D) + NORM_EPS)

        def scaled(j, _):
            normed_ref[j] = narrow(wide(noisy_ref[j]) * scale)
            return 0

        lax.fori_loop(0, 8, scaled, 0)

    def project(weights_ref):
        total_ref[...] = jnp.zeros_like(total_ref)

        def add(j, _):
            rows = pl.ds(pl.multiple_of(j * BLOCK, BLOCK), BLOCK)
            total_ref[...] += dot(normed_ref[j], weights_ref[0, rows, :])
            return 0

        lax.fori_loop(0, 8, add, 0)
        qkv_ref[step] = narrow(total_ref[...])

    @pl.when((net == 0) & (step < 3))
    def _():
        project(own_ref)

    @pl.when((net == 1) & (step < 3))
    def _():
        project(other_ref)

    @pl.when(step == 3)
    def _():
        sign = jnp.where(net == 0, sign_ref[0], -sign_ref[0])
        for head in range(BLOCK // HEAD_DIM):
            lanes = slice(head * HEAD_DIM, (head + 1) * HEAD_DIM)
            scores = dot(qkv_ref[0, :, lanes], qkv_ref[1, :, lanes], 1, 1) * HEAD_DIM ** (-0.5)
            expo = jnp.exp(scores)
            probs = narrow(expo / jnp.sum(expo, axis=-1, keepdims=True))
            attended = dot(probs, qkv_ref[2, :, lanes])
            mix_ref[net, :, lanes] = narrow(wide(narrow(attended)) * sign)

    @pl.when((net == 1) & (step == 3))
    def _():
        def emit(j, _):
            columns = pl.ds(pl.multiple_of(j * BLOCK, BLOCK), BLOCK)
            gap_ref[j] = narrow(
                dot(mix_ref[0], out_own_ref[:, columns])
                + dot(mix_ref[1], out_other_ref[:, columns])
            )
            return 0

        lax.fori_loop(0, 8, emit, 0)


def score_gap_parts(sign, noisy_all, qkv_own, qkv_other, out_own, out_other):
    weights = (1, D, BLOCK)
    whole = (BLOCK, D)
    once = pl.Buffered(1)
    return pl.pallas_call(
        score_kernel,
        out_shape=jax.ShapeDtypeStruct((8, SEQ, BLOCK), jnp.bfloat16),
        grid=(2, 4),
        in_specs=[
            pl.BlockSpec(memory_space=pltpu.SMEM),
            pl.BlockSpec((8, SEQ, BLOCK), lambda n, s: (0, 0, 0), pipeline_mode=once),
            pl.BlockSpec(weights, lambda n, s: (jnp.where(n == 0, jnp.minimum(s, 2), 2), 0, 0)),
            pl.BlockSpec(weights, lambda n, s: (jnp.where(n == 1, jnp.minimum(s, 2), 0), 0, 0)),
            pl.BlockSpec(whole, lambda n, s: (0, 0), pipeline_mode=once),
            pl.BlockSpec(whole, lambda n, s: (0, 0), pipeline_mode=once),
        ],
        out_specs=pl.BlockSpec((8, SEQ, BLOCK), lambda n, s: (0, 0, 0)),
        scratch_shapes=[
            pltpu.VMEM((8, SEQ, BLOCK), jnp.bfloat16),
            pltpu.VMEM((3, SEQ, BLOCK), jnp.bfloat16),
            pltpu.VMEM((SEQ, BLOCK), jnp.float32),
            pltpu.VMEM((2, SEQ, BLOCK), jnp.bfloat16),
        ],
        compiler_params=pltpu.CompilerParams(
            dimension_semantics=("arbitrary", "arbitrary"), vmem_limit_bytes=40 << 20
        ),
        cost_estimate=pl.CostEstimate(
            flops=5_000_000_000, bytes_accessed=22_000_000, transcendentals=400_000
        ),
        name="score_gap_parts",
    )(sign, noisy_all, qkv_own, qkv_other, out_own, out_other)


def per_device(noise_seeds, timestep_ids, gen_up, gen_down, score_qkv, score_out):
    group, x, zh = (lax.axis_index(a) for a in SAMPLES)
    y, zl = (lax.axis_index(a) for a in MODEL)
    seed = noise_seeds[0]

    down_shard = gen_down.T
    both_near = direct_gather(jnp.concatenate([gen_up, down_shard]), "x")
    up_z = direct_gather(gen_up, "zh")
    down_z = direct_gather(down_shard, "zh")
    up_rest = ring_gather(jnp.concatenate(up_z[1:]), "x")
    down_rest = ring_gather(jnp.concatenate(down_z[1:]), "x")

    def in_order(near, rest):
        first, last = near[SHARD:], rest[: 2 * SHARD]
        return lax.dynamic_slice_in_dim(
            jnp.concatenate([first, rest, first, last]), ((4 - zh) & 3) * SHARD, BLOCK, 0
        )

    up_own = [jnp.concatenate([a[:SHARD], b]) for a, b in zip(both_near, up_rest)]
    up_other = [hop(block, "group", 1) for block in up_own]
    down_own = [in_order(a, b) for a, b in zip(both_near, down_rest)]
    down_other = [hop(block, "group", 1) for block in down_own]
    qkv_own, out_own = score_qkv[0], score_out[0]
    qkv_other = hop(qkv_own, "group", 1)
    out_other = hop(out_own, "group", 1)

    index = lax.iota(jnp.int32, D)
    feature = (
        ((((index // 1536) ^ group) * 4 + ((index // BLOCK + x) & 3)) * 4
        + ((index // SHARD + zh) & 3)) * SHARD
        + index % SHARD
    )
    normed = lax.optimization_barrier(narrow(rms_norm(hashed(seed, 0, feature, SEQ))))
    normed_crossed = hop(normed[:, 1536:], "group", 1)
    normed_pair = jnp.concatenate([normed[:, :1536], normed_crossed])
    before = sum(
        dot(normed[:, k * BLOCK : (k + 1) * BLOCK], block)
        for k, block in enumerate(up_own + up_other)
    )
    hidden = narrow(jax.nn.gelu(before, approximate=True))
    hidden_pair = jnp.concatenate([hidden, hop(hidden, "group", 1)])

    down_all = down_own + down_other
    owners = [(group ^ (k // 4)) * 4 + ((x + k) & 3) for k in range(8)]
    partial = jnp.zeros((8, SEQ, BLOCK), jnp.bfloat16)
    for owner, block in zip(owners, down_all):
        partial = lax.dynamic_update_index_in_dim(
            partial, narrow(dot(hidden, block, 1, 1)), owner, 0
        )
    mixed = model_scatter(partial)
    local = lax.iota(jnp.int32, BLOCK) + (y * 2 + zl) * BLOCK
    shift = (timestep_ids[0].astype(jnp.float32) + 0.5) / STEPS
    latent = narrow(hashed(seed, 0, local, SEQ) + mixed)
    fresh = hashed(seed, 1, local, SEQ)
    noisy = narrow((1.0 - shift) * wide(latent) + shift * fresh)

    noisy_all = model_gather(noisy)
    sign = wide(2 * group - 1)[None]
    gap_parts = score_gap_parts(sign, noisy_all, qkv_own, qkv_other, out_own, out_other)
    gap = narrow(model_scatter(gap_parts))

    gap_abs = model_gather(gap)
    crossed = hop(lax.dynamic_slice_in_dim(gap_abs, (1 - group) * 4, 4, 0), "group", 1)
    kept = lax.dynamic_slice_in_dim(gap_abs, group * 4, 4, 0)
    gap_pair = jnp.concatenate([kept, crossed], axis=1)
    down_grads = [
        narrow(dot(pick(gap_pair, (x + dx) & 3), hidden_pair, 0, 0) / BATCH) for dx in range(4)
    ]
    down_sum = narrow(ring_scatter(down_grads, "x")).reshape(4, SHARD, FF_LOCAL)
    grad_down = narrow(direct_scatter([pick(down_sum, (zh + dz) & 3) for dz in range(4)], "zh")).T

    slope = sum(
        dot(pick(gap_abs, owner), block)
        for owner, block in zip(owners, down_all)
    )
    change = narrow(slope * gelu_slope(before))
    change_pair = jnp.concatenate([change, hop(change, "group", 1)])
    up_grads = [
        narrow(dot(normed_pair[:, dx * BLOCK : (dx + 1) * BLOCK], change_pair, 0, 0) / BATCH)
        for dx in range(4)
    ]
    up_sum = narrow(ring_scatter(up_grads, "x")).reshape(4, SHARD, FF_LOCAL)
    grad_up = narrow(direct_scatter([up_sum[dz] for dz in range(4)], "zh"))
    return (latent[None], gap[None], grad_up, grad_down)


def solution(mesh):
    split = Mesh(
        mesh.devices.reshape(mesh.shape["group"], 4, 4, 4, 2), ("group", "x", "zh", "y", "zl")
    )
    in_specs = (
        P(SAMPLES),
        P(SAMPLES),
        P(SAMPLES, MODEL),
        P(MODEL, SAMPLES),
        P("group", None, None, MODEL),
        P("group", MODEL, None),
    )
    out_specs = (
        P(SAMPLES, None, MODEL),
        P(SAMPLES, None, MODEL),
        P(SAMPLES, MODEL),
        P(MODEL, SAMPLES),
    )
    return jax.shard_map(
        per_device, mesh=split, in_specs=in_specs, out_specs=out_specs, check_vma=False
    )
```

```python
import jax
import jax.numpy as jnp
from jax import lax
from jax.experimental import pallas as pl
from jax.experimental.pallas import tpu as pltpu
from jax.sharding import Mesh
from jax.sharding import PartitionSpec as P


D = 3072
FF_LOCAL = 768
HEAD_DIM = 128
SEQ = 256
STEPS = 1000
BATCH = 32
SHARD = 96
BLOCK = 384
SAMPLES = ("group", "x", "zh")
MODEL = ("y", "zl")

NORM_EPS = 1e-06
ROOT_THREE = 1.7320508
GELU_SCALE = 0.7978845608


def hop(value, axis, step):
    n = lax.axis_size(axis)
    return lax.ppermute(value, axis, [(i, (i + step) % n) for i in range(n)])


def wide(value):
    return value.astype(jnp.float32)


def narrow(value):
    return value.astype(jnp.bfloat16)


def direct_gather(block, axis):
    return [block] + [hop(block, axis, -k) for k in (1, 2, 3)]


def ring_gather(block, axis):
    half = block.shape[0] // 2
    left = hop(block, axis, 1)
    right = hop(block, axis, -1)
    far_top = hop(left[:half], axis, 1)
    far_bottom = hop(right[half:], axis, -1)
    return [block, right, far_top, far_bottom, left]


def direct_scatter(parts, axis):
    return wide(parts[0]) + sum(wide(hop(parts[k], axis, k)) for k in (1, 3, 2))


def ring_scatter(parts, axis):
    own, right, far, left = parts
    half = own.shape[0] // 2
    for_right = hop(far[:half], axis, 1)
    for_left = hop(far[half:], axis, -1)
    right = jnp.concatenate([narrow(wide(right[:half]) + wide(for_right)), right[half:]])
    left = jnp.concatenate([left[:half], narrow(wide(left[half:]) + wide(for_left))])
    from_left = hop(right, axis, 1)
    from_right = hop(left, axis, -1)
    return wide(own) + wide(from_left) + wide(from_right)


def exchange(parts):
    return lax.all_to_all(parts, MODEL, 0, 0, tiled=True)


def pick(stack, index):
    return lax.dynamic_index_in_dim(stack, index, 0, keepdims=False)


def finish(mixing):
    mixing = mixing ^ mixing >> 15
    mixing = mixing * 1274126177
    mixing = mixing ^ mixing >> 13
    mixing = mixing * 1911520717
    mixing = mixing ^ mixing >> 16
    level = (mixing >> 7 & 65535).astype(jnp.float32)
    return ((level + 0.5) * (2.0 / 65536.0) - 1.0) * ROOT_THREE


def dot(left, right, left_dim=1, right_dim=0):
    return lax.dot_general(
        left, right, (((left_dim,), (right_dim,)), ((), ())), preferred_element_type=jnp.float32
    )


VMEM = pl.BlockSpec(memory_space=pltpu.VMEM)
SMEM = pl.BlockSpec(memory_space=pltpu.SMEM)
HBM = pl.BlockSpec(memory_space=pl.ANY)


def array(*shape, kind=jnp.bfloat16):
    return jax.ShapeDtypeStruct(shape, kind)


def local_call(kernel, ins, outs, flops, moved, scratch=(), limit=40):
    return pl.pallas_call(
        kernel,
        out_shape=outs,
        in_specs=ins,
        out_specs=jax.tree.map(lambda _: VMEM, outs),
        scratch_shapes=scratch,
        compiler_params=pltpu.CompilerParams(vmem_limit_bytes=limit << 20),
        cost_estimate=pl.CostEstimate(flops=flops, bytes_accessed=moved, transcendentals=0),
    )


def lane_chunk(c):
    return pl.ds(pl.multiple_of(c * 256, 256), 256)


def row_tile(i):
    return pl.ds(pl.multiple_of(i * 16, 16), 16)


def noise_kernel(seed_ref, feature_ref, own_ref, crossed_ref):
    start = seed_ref[0] * 747796405

    def tile(i, _):
        tokens = lax.broadcasted_iota(jnp.int32, (16, D), 0) + i * 16
        noise = finish(start + tokens * 1103515245 + feature_ref[...])
        scale = lax.rsqrt(jnp.mean(noise * noise, axis=-1, keepdims=True) + NORM_EPS)
        normed = narrow(noise * scale)
        own_ref[row_tile(i), :] = normed[:, : D // 2]
        crossed_ref[row_tile(i), :] = normed[:, D // 2 :]
        return 0

    lax.fori_loop(0, SEQ // 16, tile, 0)


def up_kernel(own_ref, crossed_ref, n0, n1, n2, n3, r0, r1, far_top, far_bottom, r3, here, away):
    blocks = ((n0, (r0,)), (n1, (r1,)), (n2, (far_top, far_bottom)), (n3, (r3,)))

    def columns(c, _):
        lanes = lane_chunk(c)
        weights = [
            jnp.concatenate([near[:SHARD, lanes]] + [piece[:, lanes] for piece in rest])
            for near, rest in blocks
        ]
        for normed, total in ((own_ref, here), (crossed_ref, away)):
            total[:, lanes] = sum(
                dot(normed[:, k * BLOCK : (k + 1) * BLOCK], block)
                for k, block in enumerate(weights)
            )
        return 0

    lax.fori_loop(0, FF_LOCAL // 256, columns, 0)


def hidden_kernel(here, arrived, before_ref, hidden_ref):
    def tile(i, _):
        rows = row_tile(i)
        value = here[rows, :] + arrived[rows, :]
        before_ref[rows, :] = value
        bend = jnp.tanh(GELU_SCALE * (value + 0.044715 * (value * value * value)))
        hidden_ref[rows, :] = narrow(0.5 * value * (1.0 + bend))
        return 0

    lax.fori_loop(0, SEQ // 16, tile, 0)


def down_kernel(
    at_ref, hidden_ref, crossed_ref, n0, n1, n2, n3, r0, r1, far_top, far_bottom, r3,
    down_ref, parts_ref, away_ref,
):
    group, x, zh = at_ref[0], at_ref[1], at_ref[2]
    for dx, (near, rest) in enumerate(((n0, r0), (n1, r1), (n2, None), (n3, r3))):
        spot = (x + dx) & 3
        for dz in range(4):
            base = pl.multiple_of(((zh + dz) & 3) * SHARD, 32)
            rows = pl.ds(base, SHARD)
            if dz == 0:
                down_ref[spot, rows, :] = near[SHARD:, :]
            elif rest is not None:
                down_ref[spot, rows, :] = rest[(dz - 1) * SHARD : dz * SHARD, :]
            elif dz == 1:
                down_ref[spot, rows, :] = far_top[:SHARD, :]
            elif dz == 2:
                half = SHARD // 2
                down_ref[spot, pl.ds(base, half), :] = far_top[SHARD:, :]
                low = pl.multiple_of(base + half, 16)
                down_ref[spot, pl.ds(low, half), :] = far_bottom[:half, :]
            else:
                down_ref[spot, rows, :] = far_bottom[SHARD // 2 :, :]

    def block(k, _):
        weights = down_ref[k]
        parts_ref[group * 4 + k] = narrow(dot(hidden_ref[...], weights, 1, 1))
        away_ref[k] = narrow(dot(crossed_ref[...], weights, 1, 1))
        return 0

    lax.fori_loop(0, 4, block, 0)


def score_kernel(
    sign_ref, noisy_ref, own_hbm, other_hbm, out_own_hbm, out_other_hbm, gap_ref,
    qkv_w, out_w, normed_ref, qkv_ref, mix_ref, qkv_sem, out_sem,
):
    loads = []
    for net, (source, out_source) in enumerate(
        ((own_hbm, out_own_hbm), (other_hbm, out_other_hbm))
    ):
        for k in range(3):
            loads.append(
                pltpu.make_async_copy(
                    source.at[k], qkv_w.at[net * 3 + k], qkv_sem.at[net * 3 + k]
                )
            )
        loads.append(pltpu.make_async_copy(out_source, out_w.at[net], out_sem.at[net]))
    for k in (0, 1, 2, 4, 5, 6, 3, 7):
        loads[k].start()

    def norm(i, _):
        rows = row_tile(i)
        blocks = [wide(noisy_ref[j, rows, :]) for j in range(8)]
        total = sum(jnp.sum(block * block, axis=-1, keepdims=True) for block in blocks)
        scale = lax.rsqrt(total * (1.0 / D) + NORM_EPS)
        for j in range(8):
            normed_ref[rows, j * BLOCK : (j + 1) * BLOCK] = narrow(blocks[j] * scale)
        return 0

    lax.fori_loop(0, SEQ // 16, norm, 0)

    def network(net, _):
        for own in range(2):

            @pl.when(net == own)
            def _():
                for k in range(3):
                    loads[own * 4 + k].wait()

        def project(k, _):
            qkv_ref[k] = narrow(dot(normed_ref[...], qkv_w[net * 3 + k]))
            return 0

        lax.fori_loop(0, 3, project, 0)
        sign = jnp.where(net == 0, sign_ref[0], -sign_ref[0])

        def attend(head, _):
            lanes = pl.ds(pl.multiple_of(head * HEAD_DIM, HEAD_DIM), HEAD_DIM)
            scores = dot(qkv_ref[0, :, lanes], qkv_ref[1, :, lanes], 1, 1) * HEAD_DIM ** (-0.5)
            expo = jnp.exp(scores)
            probs = narrow(expo / jnp.sum(expo, axis=-1, keepdims=True))
            attended = dot(probs, qkv_ref[2, :, lanes])
            mix_ref[net, :, lanes] = narrow(wide(narrow(attended)) * sign)
            return 0

        lax.fori_loop(0, BLOCK // HEAD_DIM, attend, 0)
        return 0

    lax.fori_loop(0, 2, network, 0)
    loads[3].wait()
    loads[7].wait()

    def emit(j, _):
        columns = pl.ds(pl.multiple_of(j * 2 * BLOCK, 2 * BLOCK), 2 * BLOCK)
        both = narrow(
            dot(mix_ref[0], out_w[0, :, columns]) + dot(mix_ref[1], out_w[1, :, columns])
        )
        gap_ref[2 * j] = both[:, :BLOCK]
        gap_ref[2 * j + 1] = both[:, BLOCK:]
        return 0

    lax.fori_loop(0, 4, emit, 0)


def slope_kernel(at_ref, gap_ref, crossed_ref, down_ref, here, away):
    group = at_ref[0]

    def columns(c, _):
        lanes = lane_chunk(c)
        here[:, lanes] = sum(dot(gap_ref[group * 4 + k], down_ref[k, :, lanes]) for k in range(4))
        away[:, lanes] = sum(dot(crossed_ref[k], down_ref[k, :, lanes]) for k in range(4))
        return 0

    lax.fori_loop(0, FF_LOCAL // 256, columns, 0)


def change_kernel(here, arrived, before_ref, change_ref):
    def tile(i, _):
        rows = row_tile(i)
        value = before_ref[rows, :]
        square = value * value
        bend = jnp.tanh(GELU_SCALE * (value + 0.044715 * square * value))
        turn = 0.5 * (1.0 + bend) + 0.5 * value * (1.0 - bend * bend) * GELU_SCALE * (
            1.0 + 3.0 * 0.044715 * square
        )
        change_ref[rows, :] = narrow((here[rows, :] + arrived[rows, :]) * turn)
        return 0

    lax.fori_loop(0, SEQ // 16, tile, 0)


def down_grad_kernel(at_ref, gap_ref, gap_crossed_ref, hidden_ref, hidden_crossed_ref, grad_ref):
    group, x = at_ref[0], at_ref[1]

    def block(k, _):
        spot = (x + k) & 3
        grad_ref[k] = narrow(
            (
                dot(gap_ref[group * 4 + spot], hidden_ref[...], 0, 0)
                + dot(gap_crossed_ref[spot], hidden_crossed_ref[...], 0, 0)
            )
            * (1.0 / BATCH)
        )
        return 0

    lax.fori_loop(0, 4, block, 0)


def up_grad_kernel(own_ref, own_crossed_ref, change_ref, change_crossed_ref, grad_ref):
    def block(k, _):
        lanes = pl.ds(pl.multiple_of(k * BLOCK, BLOCK), BLOCK)
        grad_ref[k] = narrow(
            (
                dot(own_ref[:, lanes], change_ref[...], 0, 0)
                + dot(own_crossed_ref[:, lanes], change_crossed_ref[...], 0, 0)
            )
            * (1.0 / BATCH)
        )
        return 0

    lax.fori_loop(0, 4, block, 0)


def latent_kernel(ids_ref, shift_ref, feature_ref, parts_ref, latent_ref, noisy_ref):
    start = ids_ref[0] * 747796405
    shift = shift_ref[0]

    def tile(i, _):
        rows = row_tile(i)
        tokens = lax.broadcasted_iota(jnp.int32, (16, BLOCK), 0) + i * 16
        mixing = start + tokens * 1103515245 + feature_ref[...]
        mixed = sum(wide(parts_ref[j, rows, :]) for j in range(8))
        latent = narrow(finish(mixing) + mixed)
        latent_ref[rows, :] = latent
        noisy = narrow((1.0 - shift) * wide(latent) + shift * finish(mixing + 374761393))
        for j in range(8):
            noisy_ref[j, rows, :] = noisy
        return 0

    lax.fori_loop(0, SEQ // 16, tile, 0)


def gap_kernel(parts_ref, gap_ref, copies_ref):
    def tile(i, _):
        rows = row_tile(i)
        gap = narrow(sum(wide(parts_ref[j, rows, :]) for j in range(8)))
        gap_ref[rows, :] = gap
        for j in range(8):
            copies_ref[j, rows, :] = gap
        return 0

    lax.fori_loop(0, SEQ // 16, tile, 0)


def swap(value):
    return hop(value, "group", 1)


def step(noise_seeds, timestep_ids, gen_up, gen_down, score_qkv, score_out):
    group, x, zh = (lax.axis_index(a) for a in SAMPLES)
    y, zl = (lax.axis_index(a) for a in MODEL)

    at = jnp.stack([group, x, zh])
    half_d = array(SEQ, D // 2)
    before_kind = array(SEQ, FF_LOCAL, kind=jnp.float32)
    hidden_kind = array(SEQ, FF_LOCAL)
    grad_kind = array(4, BLOCK, FF_LOCAL)
    matmul = 1_200_000_000

    down_shard = gen_down.T
    up_z = direct_gather(gen_up, "zh")
    near = direct_gather(jnp.concatenate([gen_up, down_shard]), "x")
    up_cat = jnp.concatenate(up_z[1:])
    up_rest = ring_gather(up_cat, "x")
    down_z = direct_gather(down_shard, "zh")
    down_rest = ring_gather(jnp.concatenate(down_z[1:]), "x")
    qkv_own, out_own = score_qkv[0], score_out[0]
    qkv_other, out_other = swap(qkv_own), swap(out_own)

    index = lax.iota(jnp.int32, D)
    feature = (
        (((index // 1536) ^ group) * 4 + ((index // BLOCK + x) & 3)) * 4
        + ((index // SHARD + zh) & 3)
    ) * SHARD + index % SHARD
    normed, normed_away = local_call(
        noise_kernel, [SMEM, VMEM], (half_d, half_d), 30_000_000, 1_600_000
    )(noise_seeds, (feature * 668265263)[None])
    normed_crossed = swap(normed_away)
    here, away = local_call(
        up_kernel, [VMEM] * 11, (before_kind, before_kind), matmul, 5_000_000
    )(normed, normed_crossed, *near, *up_rest)
    before, hidden = local_call(
        hidden_kernel, [VMEM] * 2, (before_kind, hidden_kind), 3_000_000, 2_800_000
    )(here, swap(away))
    hidden_crossed = swap(hidden)
    down_all, parts, parts_away = local_call(
        down_kernel,
        [SMEM] + [VMEM] * 11,
        (grad_kind, array(8, SEQ, BLOCK), array(4, SEQ, BLOCK)),
        matmul,
        8_000_000,
    )(at, hidden, hidden_crossed, *near, *down_rest)
    parts = lax.dynamic_update_slice_in_dim(parts, swap(parts_away), (1 - group) * 4, 0)

    local = lax.iota(jnp.int32, BLOCK) + (y * 2 + zl) * BLOCK
    shift = (timestep_ids[0].astype(jnp.float32) + 0.5) / STEPS
    eight_kind = array(8, SEQ, BLOCK)
    latent, noisy = local_call(
        latent_kernel, [SMEM, SMEM, VMEM, VMEM], (array(SEQ, BLOCK), eight_kind), 9_000_000, 4_000_000
    )(noise_seeds, shift[None], (local * 668265263)[None], exchange(parts))
    noisy_all = exchange(noisy)
    sign = wide(2 * group - 1)[None]
    gap_parts = local_call(
        score_kernel,
        [SMEM, VMEM] + [HBM] * 4,
        array(8, SEQ, BLOCK),
        5_000_000_000,
        20_000_000,
        scratch=[
            pltpu.VMEM((6, D, BLOCK), jnp.bfloat16),
            pltpu.VMEM((2, BLOCK, D), jnp.bfloat16),
            pltpu.VMEM((SEQ, D), jnp.bfloat16),
            pltpu.VMEM((3, SEQ, BLOCK), jnp.bfloat16),
            pltpu.VMEM((2, SEQ, BLOCK), jnp.bfloat16),
            pltpu.SemaphoreType.DMA((6,)),
            pltpu.SemaphoreType.DMA((2,)),
        ],
    )(sign, noisy_all, qkv_own, qkv_other, out_own, out_other)
    gap, gap_copies = local_call(
        gap_kernel, [VMEM], (array(SEQ, BLOCK), eight_kind), 1_000_000, 4_000_000
    )(exchange(gap_parts))
    gap_all = exchange(gap_copies)
    gap_crossed = swap(lax.dynamic_slice_in_dim(gap_all, (1 - group) * 4, 4, 0))
    down_grads = local_call(down_grad_kernel, [SMEM] + [VMEM] * 4, grad_kind, matmul, 5_000_000)(
        at, gap_all, gap_crossed, hidden, hidden_crossed
    )
    down_sum = narrow(ring_scatter([down_grads[k] for k in range(4)], "x"))
    down_sum = down_sum.reshape(4, SHARD, FF_LOCAL)
    grad_down = narrow(direct_scatter([pick(down_sum, (zh + dz) & 3) for dz in range(4)], "zh")).T

    here, away = local_call(
        slope_kernel, [SMEM] + [VMEM] * 3, (before_kind, before_kind), matmul, 6_000_000
    )(at, gap_all, gap_crossed, down_all)
    change = local_call(change_kernel, [VMEM] * 3, hidden_kind, 5_000_000, 2_800_000)(
        here, swap(away), before
    )
    up_grads = local_call(up_grad_kernel, [VMEM] * 4, grad_kind, matmul, 5_000_000)(
        normed, normed_crossed, change, swap(change)
    )
    up_sum = narrow(ring_scatter([up_grads[k] for k in range(4)], "x"))
    up_sum = up_sum.reshape(4, SHARD, FF_LOCAL)
    grad_up = narrow(direct_scatter([up_sum[dz] for dz in range(4)], "zh"))
    return (latent[None], gap[None], grad_up, grad_down)


def solution(mesh):
    split = Mesh(
        mesh.devices.reshape(mesh.shape["group"], 4, 4, 4, 2), ("group", "x", "zh", "y", "zl")
    )
    in_specs = (
        P(SAMPLES),
        P(SAMPLES),
        P(SAMPLES, MODEL),
        P(MODEL, SAMPLES),
        P("group", None, None, MODEL),
        P("group", MODEL, None),
    )
    out_specs = (
        P(SAMPLES, None, MODEL),
        P(SAMPLES, None, MODEL),
        P(SAMPLES, MODEL),
        P(MODEL, SAMPLES),
    )
    return jax.shard_map(step, mesh=split, in_specs=in_specs, out_specs=out_specs, check_vma=False)
```

```python
import jax
import jax.numpy as jnp
from jax import lax
from jax.experimental import pallas as pl
from jax.experimental.pallas import tpu as pltpu
from jax.sharding import Mesh
from jax.sharding import PartitionSpec as P


D = 3072
FF_LOCAL = 768
HEAD_DIM = 128
SEQ = 256
STEPS = 1000
BATCH = 32
SHARD = 96
BLOCK = 384
SAMPLES = ("group", "x", "zh")
MODEL = ("y", "zl")

NORM_EPS = 1e-06
ROOT_THREE = 1.7320508
GELU_SCALE = 0.7978845608


def hop(value, axis, step):
    n = lax.axis_size(axis)
    return lax.ppermute(value, axis, [(i, (i + step) % n) for i in range(n)])


def wide(value):
    return value.astype(jnp.float32)


def narrow(value):
    return value.astype(jnp.bfloat16)


def direct_gather(block, axis):
    return [block] + [hop(block, axis, -k) for k in (1, 2, 3)]


def ring_gather(block, axis):
    half = block.shape[0] // 2
    left = hop(block, axis, 1)
    right = hop(block, axis, -1)
    far_top = hop(left[:half], axis, 1)
    far_bottom = hop(right[half:], axis, -1)
    return [block, right, far_top, far_bottom, left]


def direct_scatter(parts, axis):
    return wide(parts[0]) + sum(wide(hop(parts[k], axis, k)) for k in (1, 3, 2))


def ring_scatter(grads, far_top, far_bottom, shift, axis):
    for_right = hop(far_top, axis, 1)
    for_left = hop(far_bottom, axis, -1)
    part = array(BLOCK, FF_LOCAL)
    right, left = local_call(merge_kernel, [VMEM] * 3, (part, part), 500_000, 3_000_000)(
        grads, for_right, for_left
    )
    from_left = hop(right, axis, 1)
    from_right = hop(left, axis, -1)
    return local_call(
        sum_kernel, [SMEM] + [VMEM] * 3, (array(SHARD, FF_LOCAL),) * 4, 500_000, 3_000_000
    )(shift[None], grads, from_left, from_right)


def exchange(parts):
    return lax.all_to_all(parts, MODEL, 0, 0, tiled=True)


def finish(mixing):
    mixing = mixing ^ mixing >> 15
    mixing = mixing * 1274126177
    mixing = mixing ^ mixing >> 13
    mixing = mixing * 1911520717
    mixing = mixing ^ mixing >> 16
    level = (mixing >> 7 & 65535).astype(jnp.float32)
    return ((level + 0.5) * (2.0 / 65536.0) - 1.0) * ROOT_THREE


def dot(left, right, left_dim=1, right_dim=0):
    return lax.dot_general(
        left, right, (((left_dim,), (right_dim,)), ((), ())), preferred_element_type=jnp.float32
    )


VMEM = pl.BlockSpec(memory_space=pltpu.VMEM)
SMEM = pl.BlockSpec(memory_space=pltpu.SMEM)
HBM = pl.BlockSpec(memory_space=pltpu.HBM)


def array(*shape, kind=jnp.bfloat16):
    return jax.ShapeDtypeStruct(shape, kind)


def local_call(kernel, ins, outs, flops, moved, scratch=(), limit=40, to=None):
    return pl.pallas_call(
        kernel,
        out_shape=outs,
        in_specs=ins,
        out_specs=to or jax.tree.map(lambda _: VMEM, outs),
        scratch_shapes=scratch,
        compiler_params=pltpu.CompilerParams(vmem_limit_bytes=limit << 20),
        cost_estimate=pl.CostEstimate(flops=flops, bytes_accessed=moved, transcendentals=0),
    )


def lane_chunk(c):
    return pl.ds(pl.multiple_of(c * 256, 256), 256)


def row_tile(i):
    return pl.ds(pl.multiple_of(i * 16, 16), 16)


def noise_kernel(seed_ref, feature_ref, own_ref, crossed_ref):
    start = seed_ref[0] * 747796405

    def tile(i, _):
        tokens = lax.broadcasted_iota(jnp.int32, (16, D), 0) + i * 16
        noise = finish(start + tokens * 1103515245 + feature_ref[...])
        scale = lax.rsqrt(jnp.mean(noise * noise, axis=-1, keepdims=True) + NORM_EPS)
        normed = narrow(noise * scale)
        own_ref[row_tile(i), :] = normed[:, : D // 2]
        crossed_ref[row_tile(i), :] = normed[:, D // 2 :]
        return 0

    lax.fori_loop(0, SEQ // 16, tile, 0)


def up_kernel(own_ref, crossed_ref, n0, n1, n2, n3, r0, r1, far_top, far_bottom, r3, here, away):
    blocks = ((n0, (r0,)), (n1, (r1,)), (n2, (far_top, far_bottom)), (n3, (r3,)))

    def columns(c, _):
        lanes = lane_chunk(c)
        weights = [
            jnp.concatenate([near[:SHARD, lanes]] + [piece[:, lanes] for piece in rest])
            for near, rest in blocks
        ]
        for normed, total in ((own_ref, here), (crossed_ref, away)):
            total[:, lanes] = sum(
                dot(normed[:, k * BLOCK : (k + 1) * BLOCK], block)
                for k, block in enumerate(weights)
            )
        return 0

    lax.fori_loop(0, FF_LOCAL // 256, columns, 0)


def hidden_kernel(here, arrived, before_ref, hidden_ref):
    def tile(i, _):
        rows = row_tile(i)
        value = here[rows, :] + arrived[rows, :]
        before_ref[rows, :] = value
        bend = jnp.tanh(GELU_SCALE * (value + 0.044715 * (value * value * value)))
        hidden_ref[rows, :] = narrow(0.5 * value * (1.0 + bend))
        return 0

    lax.fori_loop(0, SEQ // 16, tile, 0)


def merge_kernel(grads_ref, for_right, for_left, right_ref, left_ref):
    half = BLOCK // 2

    def tile(i, _):
        rows = row_tile(i)
        low = pl.ds(pl.multiple_of(half + i * 16, 16), 16)
        right_ref[rows, :] = narrow(wide(grads_ref[1, rows, :]) + wide(for_right[rows, :]))
        right_ref[low, :] = grads_ref[1, low, :]
        left_ref[rows, :] = grads_ref[3, rows, :]
        left_ref[low, :] = narrow(wide(grads_ref[3, low, :]) + wide(for_left[rows, :]))
        return 0

    lax.fori_loop(0, half // 16, tile, 0)


def sum_kernel(shift_ref, grads_ref, from_left, from_right, *shards):
    for dz, shard in enumerate(shards):
        base = ((shift_ref[0] + dz) & 3) * SHARD

        def tile(i, _):
            rows = pl.ds(pl.multiple_of(base + i * 16, 16), 16)
            shard[row_tile(i), :] = narrow(
                wide(grads_ref[0, rows, :]) + wide(from_left[rows, :]) + wide(from_right[rows, :])
            )
            return 0

        lax.fori_loop(0, SHARD // 16, tile, 0)


EARLY = (0, 1, 3)


def down_early_kernel(
    at_ref, hidden_ref, crossed_ref, n0, n1, n3, r0, r1, r3, down_ref, here_ref, away_ref
):
    for i, (near, rest) in enumerate(((n0, r0), (n1, r1), (n3, r3))):
        for dz in range(4):
            rows = pl.ds(pl.multiple_of(((at_ref[2] + dz) & 3) * SHARD, 32), SHARD)
            down_ref[i, rows, :] = (
                near[SHARD:, :] if dz == 0 else rest[(dz - 1) * SHARD : dz * SHARD, :]
            )

    def block(i, _):
        here_ref[i] = narrow(dot(hidden_ref[...], down_ref[i], 1, 1))
        away_ref[i] = narrow(dot(crossed_ref[...], down_ref[i], 1, 1))
        return 0

    lax.fori_loop(0, 3, block, 0)


def down_far_kernel(
    at_ref, hidden_ref, crossed_ref, n2, far_top, far_bottom, here_ref, arrived_ref,
    down_ref, parts_ref, away_ref,
):
    group, x, zh = at_ref[0], at_ref[1], at_ref[2]
    half = SHARD // 2
    for dz, pieces in enumerate(
        (
            (n2[SHARD : SHARD + half, :], n2[SHARD + half :, :]),
            (far_top[:half, :], far_top[half:SHARD, :]),
            (far_top[SHARD:, :], far_bottom[:half, :]),
            (far_bottom[half:SHARD, :], far_bottom[SHARD:, :]),
        )
    ):
        base = ((zh + dz) & 3) * SHARD
        for k, piece in enumerate(pieces):
            down_ref[pl.ds(pl.multiple_of(base + k * half, 16), half), :] = piece
    away_ref[...] = narrow(dot(crossed_ref[...], down_ref[...], 1, 1))
    parts_ref[group * 4 + ((x + 2) & 3)] = narrow(dot(hidden_ref[...], down_ref[...], 1, 1))
    for i, dx in enumerate(EARLY):
        parts_ref[group * 4 + ((x + dx) & 3)] = here_ref[i]
        parts_ref[(1 - group) * 4 + ((x + dx) & 3)] = arrived_ref[i]


def fetch_kernel(own_hbm, other_hbm, out_own_hbm, out_other_hbm, qkv_w, out_w, sems):
    loads = [
        pltpu.make_async_copy(own_hbm, qkv_w.at[:3], sems.at[0]),
        pltpu.make_async_copy(other_hbm, qkv_w.at[3:], sems.at[1]),
        pltpu.make_async_copy(out_own_hbm, out_w.at[0], sems.at[2]),
        pltpu.make_async_copy(out_other_hbm, out_w.at[1], sems.at[3]),
    ]
    for load in loads:
        load.start()
    for load in loads:
        load.wait()


def score_kernel(
    sign_ref, noisy_ref, qkv_w, out_w, gap_ref, normed_ref, qkv_ref, mix_ref
):
    def norm(i, _):
        rows = row_tile(i)
        blocks = [wide(noisy_ref[j, rows, :]) for j in range(8)]
        total = sum(jnp.sum(block * block, axis=-1, keepdims=True) for block in blocks)
        scale = lax.rsqrt(total * (1.0 / D) + NORM_EPS)
        for j in range(8):
            normed_ref[rows, j * BLOCK : (j + 1) * BLOCK] = narrow(blocks[j] * scale)
        return 0

    lax.fori_loop(0, SEQ // 16, norm, 0)

    def network(net, _):
        def project(k, _):
            qkv_ref[k] = narrow(dot(normed_ref[...], qkv_w[net * 3 + k]))
            return 0

        lax.fori_loop(0, 3, project, 0)
        sign = jnp.where(net == 0, sign_ref[0], -sign_ref[0])

        def attend(head, _):
            lanes = pl.ds(pl.multiple_of(head * HEAD_DIM, HEAD_DIM), HEAD_DIM)
            scores = dot(qkv_ref[0, :, lanes], qkv_ref[1, :, lanes], 1, 1) * HEAD_DIM ** (-0.5)
            expo = jnp.exp(scores)
            probs = narrow(expo / jnp.sum(expo, axis=-1, keepdims=True))
            attended = dot(probs, qkv_ref[2, :, lanes])
            mix_ref[net, :, lanes] = narrow(wide(narrow(attended)) * sign)
            return 0

        lax.fori_loop(0, BLOCK // HEAD_DIM, attend, 0)
        return 0

    lax.fori_loop(0, 2, network, 0)

    def emit(j, _):
        columns = pl.ds(pl.multiple_of(j * 2 * BLOCK, 2 * BLOCK), 2 * BLOCK)
        both = narrow(
            dot(mix_ref[0], out_w[0, :, columns]) + dot(mix_ref[1], out_w[1, :, columns])
        )
        gap_ref[2 * j] = both[:, :BLOCK]
        gap_ref[2 * j + 1] = both[:, BLOCK:]
        return 0

    lax.fori_loop(0, 4, emit, 0)


def slope_kernel(at_ref, gap_ref, crossed_ref, early_ref, far_ref, here, away):
    group, x = at_ref[0], at_ref[1]
    spots = [(x + dx) & 3 for dx in (*EARLY, 2)]

    def columns(c, _):
        lanes = lane_chunk(c)
        weights = [early_ref[i, :, lanes] for i in range(3)] + [far_ref[:, lanes]]
        here[:, lanes] = sum(dot(gap_ref[group * 4 + k], w) for k, w in zip(spots, weights))
        away[:, lanes] = sum(dot(crossed_ref[k], w) for k, w in zip(spots, weights))
        return 0

    lax.fori_loop(0, FF_LOCAL // 256, columns, 0)


def change_kernel(here, arrived, before_ref, change_ref):
    def tile(i, _):
        rows = row_tile(i)
        value = before_ref[rows, :]
        square = value * value
        bend = jnp.tanh(GELU_SCALE * (value + 0.044715 * square * value))
        turn = 0.5 * (1.0 + bend) + 0.5 * value * (1.0 - bend * bend) * GELU_SCALE * (
            1.0 + 3.0 * 0.044715 * square
        )
        change_ref[rows, :] = narrow((here[rows, :] + arrived[rows, :]) * turn)
        return 0

    lax.fori_loop(0, SEQ // 16, tile, 0)


def down_grad_kernel(at_ref, gap_ref, gap_crossed_ref, hidden_ref, hidden_crossed_ref, grad_ref, top, low):
    group, x = at_ref[0], at_ref[1]

    def block(k, _):
        spot = (x + k) & 3
        grad_ref[k] = narrow(
            (
                dot(gap_ref[group * 4 + spot], hidden_ref[...], 0, 0)
                + dot(gap_crossed_ref[spot], hidden_crossed_ref[...], 0, 0)
            )
            * (1.0 / BATCH)
        )
        return 0

    lax.fori_loop(0, 4, block, 0)
    top[...] = grad_ref[2, : BLOCK // 2]
    low[...] = grad_ref[2, BLOCK // 2 :]


def up_grad_kernel(own_ref, own_crossed_ref, change_ref, change_crossed_ref, grad_ref, top, low):
    def block(k, _):
        lanes = pl.ds(pl.multiple_of(k * BLOCK, BLOCK), BLOCK)
        grad_ref[k] = narrow(
            (
                dot(own_ref[:, lanes], change_ref[...], 0, 0)
                + dot(own_crossed_ref[:, lanes], change_crossed_ref[...], 0, 0)
            )
            * (1.0 / BATCH)
        )
        return 0

    lax.fori_loop(0, 4, block, 0)
    top[...] = grad_ref[2, : BLOCK // 2]
    low[...] = grad_ref[2, BLOCK // 2 :]


def latent_kernel(ids_ref, shift_ref, feature_ref, parts_ref, latent_ref, noisy_ref):
    start = ids_ref[0] * 747796405
    shift = shift_ref[0]

    def tile(i, _):
        rows = row_tile(i)
        tokens = lax.broadcasted_iota(jnp.int32, (16, BLOCK), 0) + i * 16
        mixing = start + tokens * 1103515245 + feature_ref[...]
        mixed = sum(wide(parts_ref[j, rows, :]) for j in range(8))
        latent = narrow(finish(mixing) + mixed)
        latent_ref[rows, :] = latent
        noisy = narrow((1.0 - shift) * wide(latent) + shift * finish(mixing + 374761393))
        for j in range(8):
            noisy_ref[j, rows, :] = noisy
        return 0

    lax.fori_loop(0, SEQ // 16, tile, 0)


def gap_kernel(parts_ref, gap_ref, copies_ref):
    def tile(i, _):
        rows = row_tile(i)
        gap = narrow(sum(wide(parts_ref[j, rows, :]) for j in range(8)))
        gap_ref[rows, :] = gap
        for j in range(8):
            copies_ref[j, rows, :] = gap
        return 0

    lax.fori_loop(0, SEQ // 16, tile, 0)


def swap(value):
    return hop(value, "group", 1)


def step(noise_seeds, timestep_ids, gen_up, gen_down, score_qkv, score_out):
    group, x, zh = (lax.axis_index(a) for a in SAMPLES)
    y, zl = (lax.axis_index(a) for a in MODEL)

    at = jnp.stack([group, x, zh])
    half_d = array(SEQ, D // 2)
    before_kind = array(SEQ, FF_LOCAL, kind=jnp.float32)
    hidden_kind = array(SEQ, FF_LOCAL)
    grad_kind = array(4, BLOCK, FF_LOCAL)
    matmul = 1_200_000_000

    down_shard = gen_down.T
    up_z = direct_gather(gen_up, "zh")
    near = direct_gather(jnp.concatenate([gen_up, down_shard]), "x")
    up_cat = jnp.concatenate(up_z[1:])
    up_rest = ring_gather(up_cat, "x")
    down_z = direct_gather(down_shard, "zh")
    down_rest = ring_gather(jnp.concatenate(down_z[1:]), "x")
    qkv_own, out_own = score_qkv[0], score_out[0]
    qkv_other, out_other = swap(qkv_own), swap(out_own)

    index = lax.iota(jnp.int32, D)
    feature = (
        (((index // 1536) ^ group) * 4 + ((index // BLOCK + x) & 3)) * 4
        + ((index // SHARD + zh) & 3)
    ) * SHARD + index % SHARD
    normed, normed_away = local_call(
        noise_kernel, [SMEM, VMEM], (half_d, half_d), 30_000_000, 1_600_000
    )(noise_seeds, (feature * 668265263)[None])
    normed_crossed = swap(normed_away)
    here, away = local_call(
        up_kernel, [VMEM] * 11, (before_kind, before_kind), matmul, 5_000_000
    )(normed, normed_crossed, *near, *up_rest)
    before, hidden = local_call(
        hidden_kernel, [VMEM] * 2, (before_kind, hidden_kind), 3_000_000, 2_800_000
    )(here, swap(away))
    hidden_crossed = swap(hidden)
    three = array(3, SEQ, BLOCK)
    down_early, parts_here, parts_away = local_call(
        down_early_kernel,
        [SMEM] + [VMEM] * 8,
        (array(3, BLOCK, FF_LOCAL), three, three),
        900_000_000,
        6_000_000,
    )(
        at,
        hidden,
        hidden_crossed,
        *(near[k] for k in EARLY),
        *(down_rest[k] for k in (0, 1, 4)),
    )
    eight_kind = array(8, SEQ, BLOCK)
    down_far, parts, part_away = local_call(
        down_far_kernel,
        [SMEM] + [VMEM] * 7,
        (array(BLOCK, FF_LOCAL), eight_kind, array(SEQ, BLOCK)),
        300_000_000,
        4_000_000,
    )(at, hidden, hidden_crossed, near[2], down_rest[2], down_rest[3], parts_here, swap(parts_away))
    parts = lax.dynamic_update_index_in_dim(
        parts, swap(part_away), (1 - group) * 4 + ((x + 2) & 3), 0
    )

    local = lax.iota(jnp.int32, BLOCK) + (y * 2 + zl) * BLOCK
    shift = (timestep_ids[0].astype(jnp.float32) + 0.5) / STEPS
    latent, noisy = local_call(
        latent_kernel,
        [SMEM, SMEM, VMEM, VMEM],
        (array(SEQ, BLOCK), eight_kind),
        9_000_000,
        4_000_000,
        limit=16,
    )(noise_seeds, shift[None], (local * 668265263)[None], exchange(parts))
    noisy_all = exchange(noisy)
    qkv_both, out_both = local_call(
        fetch_kernel,
        [HBM] * 4,
        (array(6, D, BLOCK), array(2, BLOCK, D)),
        1_000_000,
        38_000_000,
        scratch=[pltpu.SemaphoreType.DMA((4,))],
        limit=44,
    )(qkv_own, qkv_other, out_own, out_other)
    sign = wide(2 * group - 1)[None]
    gap_parts = local_call(
        score_kernel,
        [SMEM] + [VMEM] * 3,
        array(8, SEQ, BLOCK),
        5_000_000_000,
        20_000_000,
        scratch=[
            pltpu.VMEM((SEQ, D), jnp.bfloat16),
            pltpu.VMEM((3, SEQ, BLOCK), jnp.bfloat16),
            pltpu.VMEM((2, SEQ, BLOCK), jnp.bfloat16),
        ],
        limit=42,
    )(sign, noisy_all, qkv_both, out_both)
    gap, gap_copies = local_call(
        gap_kernel, [VMEM], (array(SEQ, BLOCK), eight_kind), 1_000_000, 4_000_000
    )(exchange(gap_parts))
    gap_all = exchange(gap_copies)
    gap_crossed = swap(lax.dynamic_slice_in_dim(gap_all, (1 - group) * 4, 4, 0))
    grad_kinds = (grad_kind, array(BLOCK // 2, FF_LOCAL), array(BLOCK // 2, FF_LOCAL))
    down_grads = local_call(down_grad_kernel, [SMEM] + [VMEM] * 4, grad_kinds, matmul, 5_000_000)(
        at, gap_all, gap_crossed, hidden, hidden_crossed
    )
    down_shards = ring_scatter(*down_grads, zh, "x")
    grad_down = narrow(direct_scatter(down_shards, "zh")).T

    here, away = local_call(
        slope_kernel, [SMEM] + [VMEM] * 4, (before_kind, before_kind), matmul, 6_000_000
    )(at, gap_all, gap_crossed, down_early, down_far)
    change = local_call(change_kernel, [VMEM] * 3, hidden_kind, 5_000_000, 2_800_000)(
        here, swap(away), before
    )
    up_grads = local_call(up_grad_kernel, [VMEM] * 4, grad_kinds, matmul, 5_000_000)(
        normed, normed_crossed, change, swap(change)
    )
    up_shards = ring_scatter(*up_grads, jnp.int32(0), "x")
    grad_up = narrow(direct_scatter(up_shards, "zh"))
    return (latent[None], gap[None], grad_up, grad_down)


def solution(mesh):
    split = Mesh(
        mesh.devices.reshape(mesh.shape["group"], 4, 4, 4, 2), ("group", "x", "zh", "y", "zl")
    )
    in_specs = (
        P(SAMPLES),
        P(SAMPLES),
        P(SAMPLES, MODEL),
        P(MODEL, SAMPLES),
        P("group", None, None, MODEL),
        P("group", MODEL, None),
    )
    out_specs = (
        P(SAMPLES, None, MODEL),
        P(SAMPLES, None, MODEL),
        P(SAMPLES, MODEL),
        P(MODEL, SAMPLES),
    )
    return jax.shard_map(step, mesh=split, in_specs=in_specs, out_specs=out_specs, check_vma=False)
```

```python
import jax
import jax.numpy as jnp
from jax import lax
from jax.experimental import pallas as pl
from jax.experimental.pallas import tpu as pltpu
from jax.sharding import Mesh
from jax.sharding import PartitionSpec as P


D = 3072
FF_LOCAL = 768
HEAD_DIM = 128
SEQ = 256
STEPS = 1000
BATCH = 32
SHARD = 96
BLOCK = 384
SAMPLES = ("group", "x", "zh")
MODEL = ("y", "zl")

NORM_EPS = 1e-06
ROOT_THREE = 1.7320508
GELU_SCALE = 0.7978845608


def hop(value, axis, step):
    n = lax.axis_size(axis)
    return lax.ppermute(value, axis, [(i, (i + step) % n) for i in range(n)])


def wide(value):
    return value.astype(jnp.float32)


def narrow(value):
    return value.astype(jnp.bfloat16)


def direct_gather(block, axis, offsets=(1, 2, 3)):
    return [hop(block, axis, -k) for k in offsets]


def ring_gather(block, axis, ahead=None):
    half = block.shape[0] // 2
    left = hop(block, axis, 1)
    right = hop(block, axis, -1)
    top, bottom = left[:half], right[half:]
    if ahead is not None:
        top, bottom = jnp.concatenate([ahead[0], top]), jnp.concatenate([ahead[1], bottom])
    far_top = hop(top, axis, 1)
    far_bottom = hop(bottom, axis, -1)
    return [block, right, far_top, far_bottom, left]


def direct_scatter(parts, axis):
    return wide(parts[0]) + sum(wide(hop(parts[k], axis, k)) for k in (1, 3, 2))


def ring_scatter(grads, far_top, far_bottom, shift, axis):
    for_right = hop(far_top, axis, 1)
    for_left = hop(far_bottom, axis, -1)
    part = array(BLOCK, FF_LOCAL)
    right, left = local_call(merge_kernel, [VMEM] * 3, (part, part), 500_000, 3_000_000)(
        grads, for_right, for_left
    )
    from_left = hop(right, axis, 1)
    from_right = hop(left, axis, -1)
    return local_call(
        sum_kernel, [SMEM] + [VMEM] * 3, (array(SHARD, FF_LOCAL),) * 4, 500_000, 3_000_000
    )(shift[None], grads, from_left, from_right)


def exchange(parts):
    return lax.all_to_all(parts, MODEL, 0, 0, tiled=True)


def finish(mixing):
    mixing = mixing ^ mixing >> 15
    mixing = mixing * 1274126177
    mixing = mixing ^ mixing >> 13
    mixing = mixing * 1911520717
    mixing = mixing ^ mixing >> 16
    level = (mixing >> 7 & 65535).astype(jnp.float32)
    return ((level + 0.5) * (2.0 / 65536.0) - 1.0) * ROOT_THREE


def dot(left, right, left_dim=1, right_dim=0):
    return lax.dot_general(
        left, right, (((left_dim,), (right_dim,)), ((), ())), preferred_element_type=jnp.float32
    )


VMEM = pl.BlockSpec(memory_space=pltpu.VMEM)
SMEM = pl.BlockSpec(memory_space=pltpu.SMEM)
HBM = pl.BlockSpec(memory_space=pltpu.HBM)


def array(*shape, kind=jnp.bfloat16):
    return jax.ShapeDtypeStruct(shape, kind)


def local_call(kernel, ins, outs, flops, moved, scratch=(), limit=40, to=None):
    return pl.pallas_call(
        kernel,
        out_shape=outs,
        in_specs=ins,
        out_specs=to or jax.tree.map(lambda _: VMEM, outs),
        scratch_shapes=scratch,
        compiler_params=pltpu.CompilerParams(vmem_limit_bytes=limit << 20),
        cost_estimate=pl.CostEstimate(flops=flops, bytes_accessed=moved, transcendentals=0),
    )


def lane_chunk(c):
    return pl.ds(pl.multiple_of(c * 256, 256), 256)


def row_tile(i):
    return pl.ds(pl.multiple_of(i * 16, 16), 16)


def noise_kernel(seed_ref, feature_ref, own_ref, crossed_ref):
    start = seed_ref[0] * 747796405

    def tile(i, _):
        tokens = lax.broadcasted_iota(jnp.int32, (16, D), 0) + i * 16
        noise = finish(start + tokens * 1103515245 + feature_ref[...])
        scale = lax.rsqrt(jnp.mean(noise * noise, axis=-1, keepdims=True) + NORM_EPS)
        normed = narrow(noise * scale)
        own_ref[row_tile(i), :] = normed[:, : D // 2]
        crossed_ref[row_tile(i), :] = normed[:, D // 2 :]
        return 0

    lax.fori_loop(0, SEQ // 16, tile, 0)


def up_kernel(own_ref, crossed_ref, n0, n1, n3, r0, r1, far_top, far_bottom, r3, here, away):
    blocks = ((n0, r0), (n1, r1), (None, None), (n3, r3))

    def columns(c, _):
        lanes = lane_chunk(c)
        weights = [
            jnp.concatenate([near[:SHARD, lanes], rest[:, lanes]])
            if near is not None
            else jnp.concatenate([far_top[:, lanes], far_bottom[SHARD:, lanes]])
            for near, rest in blocks
        ]
        for normed, total in ((own_ref, here), (crossed_ref, away)):
            total[:, lanes] = sum(
                dot(normed[:, k * BLOCK : (k + 1) * BLOCK], block)
                for k, block in enumerate(weights)
            )
        return 0

    lax.fori_loop(0, FF_LOCAL // 256, columns, 0)


def hidden_kernel(here, arrived, before_ref, hidden_ref):
    def tile(i, _):
        rows = row_tile(i)
        value = here[rows, :] + arrived[rows, :]
        before_ref[rows, :] = value
        bend = jnp.tanh(GELU_SCALE * (value + 0.044715 * (value * value * value)))
        hidden_ref[rows, :] = narrow(0.5 * value * (1.0 + bend))
        return 0

    lax.fori_loop(0, SEQ // 16, tile, 0)


def merge_kernel(grads_ref, for_right, for_left, right_ref, left_ref):
    half = BLOCK // 2

    def tile(i, _):
        rows = row_tile(i)
        low = pl.ds(pl.multiple_of(half + i * 16, 16), 16)
        right_ref[rows, :] = narrow(wide(grads_ref[1, rows, :]) + wide(for_right[rows, :]))
        right_ref[low, :] = grads_ref[1, low, :]
        left_ref[rows, :] = grads_ref[3, rows, :]
        left_ref[low, :] = narrow(wide(grads_ref[3, low, :]) + wide(for_left[rows, :]))
        return 0

    lax.fori_loop(0, half // 16, tile, 0)


def sum_kernel(shift_ref, grads_ref, from_left, from_right, *shards):
    for dz, shard in enumerate(shards):
        base = ((shift_ref[0] + dz) & 3) * SHARD

        def tile(i, _):
            rows = pl.ds(pl.multiple_of(base + i * 16, 16), 16)
            shard[row_tile(i), :] = narrow(
                wide(grads_ref[0, rows, :]) + wide(from_left[rows, :]) + wide(from_right[rows, :])
            )
            return 0

        lax.fori_loop(0, SHARD // 16, tile, 0)


EARLY = (0, 1, 3)


def down_early_kernel(
    at_ref, hidden_ref, crossed_ref, n0, n1, n3, r0, r1, r3, down_ref, here_ref, away_ref
):
    for i, (near, rest) in enumerate(((n0, r0), (n1, r1), (n3, r3))):
        for dz in range(4):
            rows = pl.ds(pl.multiple_of(((at_ref[2] + dz) & 3) * SHARD, 32), SHARD)
            down_ref[i, rows, :] = (
                near[SHARD:, :] if dz == 0 else rest[(dz - 1) * SHARD : dz * SHARD, :]
            )

    def block(i, _):
        here_ref[i] = narrow(dot(hidden_ref[...], down_ref[i], 1, 1))
        away_ref[i] = narrow(dot(crossed_ref[...], down_ref[i], 1, 1))
        return 0

    lax.fori_loop(0, 3, block, 0)


def down_far_kernel(
    at_ref, hidden_ref, crossed_ref, own_far, far_top, far_bottom, here_ref, arrived_ref,
    down_ref, parts_ref, away_ref,
):
    group, x, zh = at_ref[0], at_ref[1], at_ref[2]
    half = SHARD // 2
    for dz, pieces in enumerate(
        (
            (own_far[:half, :], own_far[half:SHARD, :]),
            (far_top[:half, :], far_top[half:SHARD, :]),
            (far_top[SHARD:, :], far_bottom[:half, :]),
            (far_bottom[half:SHARD, :], far_bottom[SHARD:, :]),
        )
    ):
        base = ((zh + dz) & 3) * SHARD
        for k, piece in enumerate(pieces):
            down_ref[pl.ds(pl.multiple_of(base + k * half, 16), half), :] = piece
    away_ref[...] = narrow(dot(crossed_ref[...], down_ref[...], 1, 1))
    parts_ref[group * 4 + ((x + 2) & 3)] = narrow(dot(hidden_ref[...], down_ref[...], 1, 1))
    for i, dx in enumerate(EARLY):
        parts_ref[group * 4 + ((x + dx) & 3)] = here_ref[i]
        parts_ref[(1 - group) * 4 + ((x + dx) & 3)] = arrived_ref[i]


def score_kernel(
    sign_ref, noisy_ref, own_hbm, other_hbm, out_own_hbm, out_other_hbm, gap_ref,
    qkv_w, out_w, normed_ref, qkv_ref, mix_ref, qkv_sem, out_sem,
):
    loads = []
    for net, (source, out_source) in enumerate(
        ((own_hbm, out_own_hbm), (other_hbm, out_other_hbm))
    ):
        for k in range(3):
            loads.append(
                pltpu.make_async_copy(
                    source.at[k], qkv_w.at[net * 3 + k], qkv_sem.at[net * 3 + k]
                )
            )
        loads.append(pltpu.make_async_copy(out_source, out_w.at[net], out_sem.at[net]))
    for k in (0, 1, 2, 4, 5, 6, 3, 7):
        loads[k].start()

    def norm(i, _):
        rows = row_tile(i)
        blocks = [wide(noisy_ref[j, rows, :]) for j in range(8)]
        total = sum(jnp.sum(block * block, axis=-1, keepdims=True) for block in blocks)
        scale = lax.rsqrt(total * (1.0 / D) + NORM_EPS)
        for j in range(8):
            normed_ref[rows, j * BLOCK : (j + 1) * BLOCK] = narrow(blocks[j] * scale)
        return 0

    lax.fori_loop(0, SEQ // 16, norm, 0)

    def network(net, _):
        def project(k, _):
            slot = net * 3 + k
            pltpu.make_async_copy(own_hbm.at[0], qkv_w.at[slot], qkv_sem.at[slot]).wait()
            qkv_ref[k] = narrow(dot(normed_ref[...], qkv_w[slot]))
            return 0

        lax.fori_loop(0, 3, project, 0)
        sign = jnp.where(net == 0, sign_ref[0], -sign_ref[0])

        def attend(head, _):
            lanes = pl.ds(pl.multiple_of(head * HEAD_DIM, HEAD_DIM), HEAD_DIM)
            scores = dot(qkv_ref[0, :, lanes], qkv_ref[1, :, lanes], 1, 1) * HEAD_DIM ** (-0.5)
            expo = jnp.exp(scores)
            probs = narrow(expo / jnp.sum(expo, axis=-1, keepdims=True))
            attended = dot(probs, qkv_ref[2, :, lanes])
            mix_ref[net, :, lanes] = narrow(wide(narrow(attended)) * sign)
            return 0

        lax.fori_loop(0, BLOCK // HEAD_DIM, attend, 0)
        return 0

    lax.fori_loop(0, 2, network, 0)
    loads[3].wait()
    loads[7].wait()

    def emit(j, _):
        columns = pl.ds(pl.multiple_of(j * 2 * BLOCK, 2 * BLOCK), 2 * BLOCK)
        both = narrow(
            dot(mix_ref[0], out_w[0, :, columns]) + dot(mix_ref[1], out_w[1, :, columns])
        )
        gap_ref[2 * j] = both[:, :BLOCK]
        gap_ref[2 * j + 1] = both[:, BLOCK:]
        return 0

    lax.fori_loop(0, 4, emit, 0)


def slope_kernel(at_ref, gap_ref, crossed_ref, early_ref, far_ref, here, away):
    group, x = at_ref[0], at_ref[1]
    spots = [(x + dx) & 3 for dx in (*EARLY, 2)]

    def columns(c, _):
        lanes = lane_chunk(c)
        weights = [early_ref[i, :, lanes] for i in range(3)] + [far_ref[:, lanes]]
        here[:, lanes] = sum(dot(gap_ref[group * 4 + k], w) for k, w in zip(spots, weights))
        away[:, lanes] = sum(dot(crossed_ref[k], w) for k, w in zip(spots, weights))
        return 0

    lax.fori_loop(0, FF_LOCAL // 256, columns, 0)


def change_kernel(here, arrived, before_ref, change_ref):
    def tile(i, _):
        rows = row_tile(i)
        value = before_ref[rows, :]
        square = value * value
        bend = jnp.tanh(GELU_SCALE * (value + 0.044715 * square * value))
        turn = 0.5 * (1.0 + bend) + 0.5 * value * (1.0 - bend * bend) * GELU_SCALE * (
            1.0 + 3.0 * 0.044715 * square
        )
        change_ref[rows, :] = narrow((here[rows, :] + arrived[rows, :]) * turn)
        return 0

    lax.fori_loop(0, SEQ // 16, tile, 0)


def down_grad_kernel(at_ref, gap_ref, gap_crossed_ref, hidden_ref, hidden_crossed_ref, grad_ref, top, low):
    group, x = at_ref[0], at_ref[1]

    def block(k, _):
        spot = (x + k) & 3
        grad_ref[k] = narrow(
            (
                dot(gap_ref[group * 4 + spot], hidden_ref[...], 0, 0)
                + dot(gap_crossed_ref[spot], hidden_crossed_ref[...], 0, 0)
            )
            * (1.0 / BATCH)
        )
        return 0

    lax.fori_loop(0, 4, block, 0)
    top[...] = grad_ref[2, : BLOCK // 2]
    low[...] = grad_ref[2, BLOCK // 2 :]


def up_grad_kernel(own_ref, own_crossed_ref, change_ref, change_crossed_ref, grad_ref, top, low):
    def block(k, _):
        lanes = pl.ds(pl.multiple_of(k * BLOCK, BLOCK), BLOCK)
        grad_ref[k] = narrow(
            (
                dot(own_ref[:, lanes], change_ref[...], 0, 0)
                + dot(own_crossed_ref[:, lanes], change_crossed_ref[...], 0, 0)
            )
            * (1.0 / BATCH)
        )
        return 0

    lax.fori_loop(0, 4, block, 0)
    top[...] = grad_ref[2, : BLOCK // 2]
    low[...] = grad_ref[2, BLOCK // 2 :]


def latent_kernel(ids_ref, shift_ref, feature_ref, parts_ref, latent_ref, noisy_ref):
    start = ids_ref[0] * 747796405
    shift = shift_ref[0]

    def tile(i, _):
        rows = row_tile(i)
        tokens = lax.broadcasted_iota(jnp.int32, (16, BLOCK), 0) + i * 16
        mixing = start + tokens * 1103515245 + feature_ref[...]
        mixed = sum(wide(parts_ref[j, rows, :]) for j in range(8))
        latent = narrow(finish(mixing) + mixed)
        latent_ref[rows, :] = latent
        noisy = narrow((1.0 - shift) * wide(latent) + shift * finish(mixing + 374761393))
        for j in range(8):
            noisy_ref[j, rows, :] = noisy
        return 0

    lax.fori_loop(0, SEQ // 16, tile, 0)


def gap_kernel(parts_ref, gap_ref, copies_ref):
    def tile(i, _):
        rows = row_tile(i)
        gap = narrow(sum(wide(parts_ref[j, rows, :]) for j in range(8)))
        gap_ref[rows, :] = gap
        for j in range(8):
            copies_ref[j, rows, :] = gap
        return 0

    lax.fori_loop(0, SEQ // 16, tile, 0)


def swap(value):
    return hop(value, "group", 1)


def step(noise_seeds, timestep_ids, gen_up, gen_down, score_qkv, score_out):
    group, x, zh = (lax.axis_index(a) for a in SAMPLES)
    y, zl = (lax.axis_index(a) for a in MODEL)

    at = jnp.stack([group, x, zh])
    half_d = array(SEQ, D // 2)
    before_kind = array(SEQ, FF_LOCAL, kind=jnp.float32)
    hidden_kind = array(SEQ, FF_LOCAL)
    grad_kind = array(4, BLOCK, FF_LOCAL)
    matmul = 1_200_000_000

    down_shard = gen_down.T
    up_z = direct_gather(gen_up, "zh")
    both = jnp.concatenate([gen_up, down_shard])
    near_right, near_left = direct_gather(both, "x", (1, 3))
    near = [both, near_right, near_left]
    up_rest = ring_gather(jnp.concatenate(up_z), "x", (near_left[:SHARD], near_right[SHARD:]))
    down_z = direct_gather(down_shard, "zh")
    down_rest = ring_gather(jnp.concatenate(down_z), "x")
    qkv_own, out_own = score_qkv[0], score_out[0]
    qkv_other, out_other = swap(qkv_own), swap(out_own)

    index = lax.iota(jnp.int32, D)
    feature = (
        (((index // 1536) ^ group) * 4 + ((index // BLOCK + x) & 3)) * 4
        + ((index // SHARD + zh) & 3)
    ) * SHARD + index % SHARD
    normed, normed_away = local_call(
        noise_kernel, [SMEM, VMEM], (half_d, half_d), 30_000_000, 1_600_000
    )(noise_seeds, (feature * 668265263)[None])
    normed_crossed = swap(normed_away)
    here, away = local_call(
        up_kernel, [VMEM] * 10, (before_kind, before_kind), matmul, 5_000_000
    )(normed, normed_crossed, *near, *up_rest)
    before, hidden = local_call(
        hidden_kernel, [VMEM] * 2, (before_kind, hidden_kind), 3_000_000, 2_800_000
    )(here, swap(away))
    hidden_crossed = swap(hidden)
    three = array(3, SEQ, BLOCK)
    down_early, parts_here, parts_away = local_call(
        down_early_kernel,
        [SMEM] + [VMEM] * 8,
        (array(3, BLOCK, FF_LOCAL), three, three),
        900_000_000,
        6_000_000,
    )(
        at,
        hidden,
        hidden_crossed,
        *near,
        *(down_rest[k] for k in (0, 1, 4)),
    )
    eight_kind = array(8, SEQ, BLOCK)
    down_far, parts, part_away = local_call(
        down_far_kernel,
        [SMEM] + [VMEM] * 7,
        (array(BLOCK, FF_LOCAL), eight_kind, array(SEQ, BLOCK)),
        300_000_000,
        4_000_000,
    )(at, hidden, hidden_crossed, up_rest[3], down_rest[2], down_rest[3], parts_here, swap(parts_away))
    parts = lax.dynamic_update_index_in_dim(
        parts, swap(part_away), (1 - group) * 4 + ((x + 2) & 3), 0
    )

    local = lax.iota(jnp.int32, BLOCK) + (y * 2 + zl) * BLOCK
    shift = (timestep_ids[0].astype(jnp.float32) + 0.5) / STEPS
    latent, noisy = local_call(
        latent_kernel,
        [SMEM, SMEM, VMEM, VMEM],
        (array(SEQ, BLOCK), eight_kind),
        9_000_000,
        4_000_000,
        limit=16,
    )(noise_seeds, shift[None], (local * 668265263)[None], exchange(parts))
    noisy_all = exchange(noisy)
    sign = wide(2 * group - 1)[None]
    gap_parts = local_call(
        score_kernel,
        [SMEM, VMEM] + [HBM] * 4,
        array(8, SEQ, BLOCK),
        5_000_000_000,
        20_000_000,
        scratch=[
            pltpu.VMEM((6, D, BLOCK), jnp.bfloat16),
            pltpu.VMEM((2, BLOCK, D), jnp.bfloat16),
            pltpu.VMEM((SEQ, D), jnp.bfloat16),
            pltpu.VMEM((3, SEQ, BLOCK), jnp.bfloat16),
            pltpu.VMEM((2, SEQ, BLOCK), jnp.bfloat16),
            pltpu.SemaphoreType.DMA((6,)),
            pltpu.SemaphoreType.DMA((2,)),
        ],
        limit=44,
    )(sign, noisy_all, qkv_own, qkv_other, out_own, out_other)
    gap, gap_copies = local_call(
        gap_kernel, [VMEM], (array(SEQ, BLOCK), eight_kind), 1_000_000, 4_000_000
    )(exchange(gap_parts))
    gap_all = exchange(gap_copies)
    gap_crossed = swap(lax.dynamic_slice_in_dim(gap_all, (1 - group) * 4, 4, 0))
    grad_kinds = (grad_kind, array(BLOCK // 2, FF_LOCAL), array(BLOCK // 2, FF_LOCAL))
    down_grads = local_call(down_grad_kernel, [SMEM] + [VMEM] * 4, grad_kinds, matmul, 5_000_000)(
        at, gap_all, gap_crossed, hidden, hidden_crossed
    )
    down_shards = ring_scatter(*down_grads, zh, "x")
    grad_down = narrow(direct_scatter(down_shards, "zh")).T

    here, away = local_call(
        slope_kernel, [SMEM] + [VMEM] * 4, (before_kind, before_kind), matmul, 6_000_000
    )(at, gap_all, gap_crossed, down_early, down_far)
    change = local_call(change_kernel, [VMEM] * 3, hidden_kind, 5_000_000, 2_800_000)(
        here, swap(away), before
    )
    up_grads = local_call(up_grad_kernel, [VMEM] * 4, grad_kinds, matmul, 5_000_000)(
        normed, normed_crossed, change, swap(change)
    )
    up_shards = ring_scatter(*up_grads, jnp.int32(0), "x")
    grad_up = narrow(direct_scatter(up_shards, "zh"))
    return (latent[None], gap[None], grad_up, grad_down)


def solution(mesh):
    split = Mesh(
        mesh.devices.reshape(mesh.shape["group"], 4, 4, 4, 2), ("group", "x", "zh", "y", "zl")
    )
    in_specs = (
        P(SAMPLES),
        P(SAMPLES),
        P(SAMPLES, MODEL),
        P(MODEL, SAMPLES),
        P("group", None, None, MODEL),
        P("group", MODEL, None),
    )
    out_specs = (
        P(SAMPLES, None, MODEL),
        P(SAMPLES, None, MODEL),
        P(SAMPLES, MODEL),
        P(MODEL, SAMPLES),
    )
    return jax.shard_map(step, mesh=split, in_specs=in_specs, out_specs=out_specs, check_vma=False)
```

```python
import functools

import jax
import jax.numpy as jnp
from jax import lax
from jax.experimental import pallas as pl
from jax.experimental.pallas import tpu as pltpu
from jax.sharding import Mesh
from jax.sharding import PartitionSpec as P


D = 3072
FF_LOCAL = 768
HEAD_DIM = 128
SEQ = 256
STEPS = 1000
BATCH = 32
SHARD = 96
BLOCK = 384
SAMPLES = ("group", "x", "zh")
MODEL = ("y", "zl")

NORM_EPS = 1e-06
ROOT_THREE = 1.7320508
GELU_SCALE = 0.7978845608


def hop(value, axis, step):
    n = lax.axis_size(axis)
    return lax.ppermute(value, axis, [(i, (i + step) % n) for i in range(n)])


def wide(value):
    return value.astype(jnp.float32)


def narrow(value):
    return value.astype(jnp.bfloat16)


def direct_gather(block, axis, offsets=(1, 2, 3)):
    return [hop(block, axis, -k) for k in offsets]


def ring_gather(block, axis, ahead=None):
    half = block.shape[0] // 2
    left = hop(block, axis, 1)
    right = hop(block, axis, -1)
    top, bottom = left[:half], right[half:]
    if ahead is not None:
        top, bottom = jnp.concatenate([ahead[0], top]), jnp.concatenate([ahead[1], bottom])
    far_top = hop(top, axis, 1)
    far_bottom = hop(bottom, axis, -1)
    return [block, right, far_top, far_bottom, left]


def direct_scatter(parts, axis):
    return wide(parts[0]) + sum(wide(hop(parts[k], axis, k)) for k in (1, 3, 2))


def ring_scatter(grads, far_top, far_bottom, at, axis, turned):
    for_right = hop(far_top, axis, 1)
    for_left = hop(far_bottom, axis, -1)
    part = array(BLOCK, FF_LOCAL)
    right, left = local_call(merge_kernel, [VMEM] * 3, (part, part), 500_000, 3_000_000)(
        grads, for_right, for_left
    )
    from_left = hop(right, axis, 1)
    from_right = hop(left, axis, -1)
    return local_call(
        functools.partial(sum_kernel, turned=turned),
        [SMEM] + [VMEM] * 3,
        (array(SHARD, FF_LOCAL),) * 4,
        500_000,
        3_000_000,
    )(at, grads, from_left, from_right)


def exchange(parts):
    return lax.all_to_all(parts, MODEL, 0, 0, tiled=True)


def finish(mixing):
    mixing = mixing ^ mixing >> 15
    mixing = mixing * 1274126177
    mixing = mixing ^ mixing >> 13
    mixing = mixing * 1911520717
    mixing = mixing ^ mixing >> 16
    level = (mixing >> 7 & 65535).astype(jnp.float32)
    return ((level + 0.5) * (2.0 / 65536.0) - 1.0) * ROOT_THREE


def dot(left, right, left_dim=1, right_dim=0):
    return lax.dot_general(
        left, right, (((left_dim,), (right_dim,)), ((), ())), preferred_element_type=jnp.float32
    )


VMEM = pl.BlockSpec(memory_space=pltpu.VMEM)
SMEM = pl.BlockSpec(memory_space=pltpu.SMEM)
HBM = pl.BlockSpec(memory_space=pltpu.HBM)


def array(*shape, kind=jnp.bfloat16):
    return jax.ShapeDtypeStruct(shape, kind)


def local_call(kernel, ins, outs, flops, moved, scratch=(), limit=40, to=None):
    return pl.pallas_call(
        kernel,
        out_shape=outs,
        in_specs=ins,
        out_specs=to or jax.tree.map(lambda _: VMEM, outs),
        scratch_shapes=scratch,
        compiler_params=pltpu.CompilerParams(vmem_limit_bytes=limit << 20),
        cost_estimate=pl.CostEstimate(flops=flops, bytes_accessed=moved, transcendentals=0),
    )


def lane_chunk(c):
    return pl.ds(pl.multiple_of(c * 256, 256), 256)


def row_tile(i):
    return pl.ds(pl.multiple_of(i * 16, 16), 16)


def noise_kernel(seed_ref, feature_ref, own_ref, crossed_ref):
    start = seed_ref[0] * 747796405

    def tile(i, _):
        tokens = lax.broadcasted_iota(jnp.int32, (16, D), 0) + i * 16
        noise = finish(start + tokens * 1103515245 + feature_ref[...])
        scale = lax.rsqrt(jnp.mean(noise * noise, axis=-1, keepdims=True) + NORM_EPS)
        normed = narrow(noise * scale)
        own_ref[row_tile(i), :] = normed[:, : D // 2]
        crossed_ref[row_tile(i), :] = normed[:, D // 2 :]
        return 0

    lax.fori_loop(0, SEQ // 16, tile, 0)


def up_kernel(own_ref, crossed_ref, n0, n1, n3, r0, r1, far_top, far_bottom, r3, here, away):
    blocks = ((n0, r0), (n1, r1), (None, None), (n3, r3))

    def columns(c, _):
        lanes = lane_chunk(c)
        weights = [
            jnp.concatenate([near[:SHARD, lanes], rest[:, lanes]])
            if near is not None
            else jnp.concatenate([far_top[:, lanes], far_bottom[SHARD:, lanes]])
            for near, rest in blocks
        ]
        for normed, total in ((own_ref, here), (crossed_ref, away)):
            total[:, lanes] = sum(
                dot(normed[:, k * BLOCK : (k + 1) * BLOCK], block)
                for k, block in enumerate(weights)
            )
        return 0

    lax.fori_loop(0, FF_LOCAL // 256, columns, 0)


def hidden_kernel(here, arrived, before_ref, hidden_ref):
    def tile(i, _):
        rows = row_tile(i)
        value = here[rows, :] + arrived[rows, :]
        before_ref[rows, :] = value
        bend = jnp.tanh(GELU_SCALE * (value + 0.044715 * (value * value * value)))
        hidden_ref[rows, :] = narrow(0.5 * value * (1.0 + bend))
        return 0

    lax.fori_loop(0, SEQ // 16, tile, 0)


def merge_kernel(grads_ref, for_right, for_left, right_ref, left_ref):
    half = BLOCK // 2

    def tile(i, _):
        rows = row_tile(i)
        low = pl.ds(pl.multiple_of(half + i * 16, 16), 16)
        right_ref[rows, :] = narrow(wide(grads_ref[1, rows, :]) + wide(for_right[rows, :]))
        right_ref[low, :] = grads_ref[1, low, :]
        left_ref[rows, :] = grads_ref[3, rows, :]
        left_ref[low, :] = narrow(wide(grads_ref[3, low, :]) + wide(for_left[rows, :]))
        return 0

    lax.fori_loop(0, half // 16, tile, 0)


def sum_kernel(at_ref, grads_ref, from_left, from_right, *shards, turned):
    first = at_ref[2] if turned else 0
    for dz, shard in enumerate(shards):
        base = ((first + dz) & 3) * SHARD

        def tile(i, _):
            rows = pl.ds(pl.multiple_of(base + i * 16, 16), 16)
            shard[row_tile(i), :] = narrow(
                wide(grads_ref[0, rows, :]) + wide(from_left[rows, :]) + wide(from_right[rows, :])
            )
            return 0

        lax.fori_loop(0, SHARD // 16, tile, 0)


EARLY = (0, 1, 3)


def down_early_kernel(
    at_ref, hidden_ref, crossed_ref, n0, n1, n3, r0, r1, r3, down_ref, here_ref, away_ref
):
    for i, (near, rest) in enumerate(((n0, r0), (n1, r1), (n3, r3))):
        for dz in range(4):
            rows = pl.ds(pl.multiple_of(((at_ref[2] + dz) & 3) * SHARD, 32), SHARD)
            down_ref[i, rows, :] = (
                near[SHARD:, :] if dz == 0 else rest[(dz - 1) * SHARD : dz * SHARD, :]
            )

    def block(i, _):
        here_ref[i] = narrow(dot(hidden_ref[...], down_ref[i], 1, 1))
        away_ref[i] = narrow(dot(crossed_ref[...], down_ref[i], 1, 1))
        return 0

    lax.fori_loop(0, 3, block, 0)


def down_far_kernel(at_ref, crossed_ref, own_far, far_top, far_bottom, down_ref, away_ref):
    zh = at_ref[2]
    half = SHARD // 2
    for dz, pieces in enumerate(
        (
            (own_far[:half, :], own_far[half:SHARD, :]),
            (far_top[:half, :], far_top[half:SHARD, :]),
            (far_top[SHARD:, :], far_bottom[:half, :]),
            (far_bottom[half:SHARD, :], far_bottom[SHARD:, :]),
        )
    ):
        base = ((zh + dz) & 3) * SHARD
        for k, piece in enumerate(pieces):
            down_ref[pl.ds(pl.multiple_of(base + k * half, 16), half), :] = piece
    away_ref[...] = narrow(dot(crossed_ref[...], down_ref[...], 1, 1))


def parts_kernel(at_ref, hidden_ref, down_ref, here_ref, arrived_ref, parts_ref):
    group, x = at_ref[0], at_ref[1]
    parts_ref[group * 4 + ((x + 2) & 3)] = narrow(dot(hidden_ref[...], down_ref[...], 1, 1))
    for i, dx in enumerate(EARLY):
        parts_ref[group * 4 + ((x + dx) & 3)] = here_ref[i]
        parts_ref[(1 - group) * 4 + ((x + dx) & 3)] = arrived_ref[i]


def score_kernel(
    sign_ref, noisy_ref, own_hbm, other_hbm, out_own_hbm, out_other_hbm, gap_ref,
    qkv_w, out_w, normed_ref, qkv_ref, mix_ref, qkv_sem, out_sem,
):
    loads = []
    for net, (source, out_source) in enumerate(
        ((own_hbm, out_own_hbm), (other_hbm, out_other_hbm))
    ):
        for k in range(3):
            loads.append(
                pltpu.make_async_copy(
                    source.at[k], qkv_w.at[net * 3 + k], qkv_sem.at[net * 3 + k]
                )
            )
        loads.append(pltpu.make_async_copy(out_source, out_w.at[net], out_sem.at[net]))
    for k in (0, 1, 2, 4, 5, 6, 3, 7):
        loads[k].start()

    def norm(i, _):
        rows = row_tile(i)
        blocks = [wide(noisy_ref[j, rows, :]) for j in range(8)]
        total = sum(jnp.sum(block * block, axis=-1, keepdims=True) for block in blocks)
        scale = lax.rsqrt(total * (1.0 / D) + NORM_EPS)
        for j in range(8):
            normed_ref[rows, j * BLOCK : (j + 1) * BLOCK] = narrow(blocks[j] * scale)
        return 0

    lax.fori_loop(0, SEQ // 16, norm, 0)

    def network(net, _):
        def project(k, _):
            slot = net * 3 + k
            pltpu.make_async_copy(own_hbm.at[0], qkv_w.at[slot], qkv_sem.at[slot]).wait()
            qkv_ref[k] = narrow(dot(normed_ref[...], qkv_w[slot]))
            return 0

        lax.fori_loop(0, 3, project, 0)
        sign = jnp.where(net == 0, sign_ref[0], -sign_ref[0])

        def attend(head, _):
            lanes = pl.ds(pl.multiple_of(head * HEAD_DIM, HEAD_DIM), HEAD_DIM)
            scores = dot(qkv_ref[0, :, lanes], qkv_ref[1, :, lanes], 1, 1) * HEAD_DIM ** (-0.5)
            expo = jnp.exp(scores)
            probs = narrow(expo / jnp.sum(expo, axis=-1, keepdims=True))
            attended = dot(probs, qkv_ref[2, :, lanes])
            mix_ref[net, :, lanes] = narrow(wide(narrow(attended)) * sign)
            return 0

        lax.fori_loop(0, BLOCK // HEAD_DIM, attend, 0)
        return 0

    lax.fori_loop(0, 2, network, 0)
    loads[3].wait()
    loads[7].wait()

    def emit(j, _):
        columns = pl.ds(pl.multiple_of(j * 2 * BLOCK, 2 * BLOCK), 2 * BLOCK)
        both = narrow(
            dot(mix_ref[0], out_w[0, :, columns]) + dot(mix_ref[1], out_w[1, :, columns])
        )
        gap_ref[2 * j] = both[:, :BLOCK]
        gap_ref[2 * j + 1] = both[:, BLOCK:]
        return 0

    lax.fori_loop(0, 4, emit, 0)


def slope_kernel(at_ref, gap_ref, crossed_ref, early_ref, far_ref, here, away):
    group, x = at_ref[0], at_ref[1]
    spots = [(x + dx) & 3 for dx in (*EARLY, 2)]

    def columns(c, _):
        lanes = lane_chunk(c)
        weights = [early_ref[i, :, lanes] for i in range(3)] + [far_ref[:, lanes]]
        here[:, lanes] = sum(dot(gap_ref[group * 4 + k], w) for k, w in zip(spots, weights))
        away[:, lanes] = sum(dot(crossed_ref[k], w) for k, w in zip(spots, weights))
        return 0

    lax.fori_loop(0, FF_LOCAL // 256, columns, 0)


def change_kernel(here, arrived, before_ref, change_ref):
    def tile(i, _):
        rows = row_tile(i)
        value = before_ref[rows, :]
        square = value * value
        bend = jnp.tanh(GELU_SCALE * (value + 0.044715 * square * value))
        turn = 0.5 * (1.0 + bend) + 0.5 * value * (1.0 - bend * bend) * GELU_SCALE * (
            1.0 + 3.0 * 0.044715 * square
        )
        change_ref[rows, :] = narrow((here[rows, :] + arrived[rows, :]) * turn)
        return 0

    lax.fori_loop(0, SEQ // 16, tile, 0)


def down_grad_kernel(at_ref, gap_ref, gap_crossed_ref, hidden_ref, hidden_crossed_ref, grad_ref, top, low):
    group, x = at_ref[0], at_ref[1]

    def block(k, _):
        spot = (x + k) & 3
        grad_ref[k] = narrow(
            (
                dot(gap_ref[group * 4 + spot], hidden_ref[...], 0, 0)
                + dot(gap_crossed_ref[spot], hidden_crossed_ref[...], 0, 0)
            )
            * (1.0 / BATCH)
        )
        return 0

    lax.fori_loop(0, 4, block, 0)
    top[...] = grad_ref[2, : BLOCK // 2]
    low[...] = grad_ref[2, BLOCK // 2 :]


def up_grad_kernel(own_ref, own_crossed_ref, change_ref, change_crossed_ref, grad_ref, top, low):
    def block(k, _):
        lanes = pl.ds(pl.multiple_of(k * BLOCK, BLOCK), BLOCK)
        grad_ref[k] = narrow(
            (
                dot(own_ref[:, lanes], change_ref[...], 0, 0)
                + dot(own_crossed_ref[:, lanes], change_crossed_ref[...], 0, 0)
            )
            * (1.0 / BATCH)
        )
        return 0

    lax.fori_loop(0, 4, block, 0)
    top[...] = grad_ref[2, : BLOCK // 2]
    low[...] = grad_ref[2, BLOCK // 2 :]


def latent_kernel(ids_ref, shift_ref, feature_ref, parts_ref, latent_ref, noisy_ref):
    start = ids_ref[0] * 747796405
    shift = shift_ref[0]

    def tile(i, _):
        rows = row_tile(i)
        tokens = lax.broadcasted_iota(jnp.int32, (16, BLOCK), 0) + i * 16
        mixing = start + tokens * 1103515245 + feature_ref[...]
        mixed = sum(wide(parts_ref[j, rows, :]) for j in range(8))
        latent = narrow(finish(mixing) + mixed)
        latent_ref[rows, :] = latent
        noisy = narrow((1.0 - shift) * wide(latent) + shift * finish(mixing + 374761393))
        for j in range(8):
            noisy_ref[j, rows, :] = noisy
        return 0

    lax.fori_loop(0, SEQ // 16, tile, 0)


def gap_kernel(parts_ref, gap_ref, copies_ref):
    def tile(i, _):
        rows = row_tile(i)
        gap = narrow(sum(wide(parts_ref[j, rows, :]) for j in range(8)))
        gap_ref[rows, :] = gap
        for j in range(8):
            copies_ref[j, rows, :] = gap
        return 0

    lax.fori_loop(0, SEQ // 16, tile, 0)


def swap(value):
    return hop(value, "group", 1)


def step(noise_seeds, timestep_ids, gen_up, gen_down, score_qkv, score_out):
    group, x, zh = (lax.axis_index(a) for a in SAMPLES)
    y, zl = (lax.axis_index(a) for a in MODEL)

    at = jnp.stack([group, x, zh])
    half_d = array(SEQ, D // 2)
    before_kind = array(SEQ, FF_LOCAL, kind=jnp.float32)
    hidden_kind = array(SEQ, FF_LOCAL)
    grad_kind = array(4, BLOCK, FF_LOCAL)
    matmul = 1_200_000_000

    down_shard = gen_down.T
    up_z = direct_gather(gen_up, "zh")
    both = jnp.concatenate([gen_up, down_shard])
    near_right, near_left = direct_gather(both, "x", (1, 3))
    near = [both, near_right, near_left]
    up_rest = ring_gather(jnp.concatenate(up_z), "x", (near_left[:SHARD], near_right[SHARD:]))
    down_z = direct_gather(down_shard, "zh")
    down_rest = ring_gather(jnp.concatenate(down_z), "x")
    qkv_own, out_own = score_qkv[0], score_out[0]
    qkv_other, out_other = swap(qkv_own), swap(out_own)

    index = lax.iota(jnp.int32, D)
    feature = (
        (((index // 1536) ^ group) * 4 + ((index // BLOCK + x) & 3)) * 4
        + ((index // SHARD + zh) & 3)
    ) * SHARD + index % SHARD
    normed, normed_away = local_call(
        noise_kernel, [SMEM, VMEM], (half_d, half_d), 30_000_000, 1_600_000
    )(noise_seeds, (feature * 668265263)[None])
    normed_crossed = swap(normed_away)
    here, away = local_call(
        up_kernel, [VMEM] * 10, (before_kind, before_kind), matmul, 5_000_000
    )(normed, normed_crossed, *near, *up_rest)
    before, hidden = local_call(
        hidden_kernel, [VMEM] * 2, (before_kind, hidden_kind), 3_000_000, 2_800_000
    )(here, swap(away))
    hidden_crossed = swap(hidden)
    three = array(3, SEQ, BLOCK)
    down_early, parts_here, parts_away = local_call(
        down_early_kernel,
        [SMEM] + [VMEM] * 8,
        (array(3, BLOCK, FF_LOCAL), three, three),
        900_000_000,
        6_000_000,
    )(
        at,
        hidden,
        hidden_crossed,
        *near,
        *(down_rest[k] for k in (0, 1, 4)),
    )
    eight_kind = array(8, SEQ, BLOCK)
    down_far, part_away = local_call(
        down_far_kernel,
        [SMEM] + [VMEM] * 4,
        (array(BLOCK, FF_LOCAL), array(SEQ, BLOCK)),
        150_000_000,
        2_000_000,
    )(at, hidden_crossed, up_rest[3], down_rest[2], down_rest[3])
    part_arrived = swap(part_away)
    parts = local_call(
        parts_kernel, [SMEM] + [VMEM] * 4, eight_kind, 150_000_000, 4_000_000
    )(at, hidden, down_far, parts_here, swap(parts_away))
    parts = lax.dynamic_update_index_in_dim(
        parts, part_arrived, (1 - group) * 4 + ((x + 2) & 3), 0
    )

    local = lax.iota(jnp.int32, BLOCK) + (y * 2 + zl) * BLOCK
    shift = (timestep_ids[0].astype(jnp.float32) + 0.5) / STEPS
    latent, noisy = local_call(
        latent_kernel,
        [SMEM, SMEM, VMEM, VMEM],
        (array(SEQ, BLOCK), eight_kind),
        9_000_000,
        4_000_000,
        limit=16,
    )(noise_seeds, shift[None], (local * 668265263)[None], exchange(parts))
    noisy_all = exchange(noisy)
    sign = wide(2 * group - 1)[None]
    gap_parts = local_call(
        score_kernel,
        [SMEM, VMEM] + [HBM] * 4,
        array(8, SEQ, BLOCK),
        5_000_000_000,
        20_000_000,
        scratch=[
            pltpu.VMEM((6, D, BLOCK), jnp.bfloat16),
            pltpu.VMEM((2, BLOCK, D), jnp.bfloat16),
            pltpu.VMEM((SEQ, D), jnp.bfloat16),
            pltpu.VMEM((3, SEQ, BLOCK), jnp.bfloat16),
            pltpu.VMEM((2, SEQ, BLOCK), jnp.bfloat16),
            pltpu.SemaphoreType.DMA((6,)),
            pltpu.SemaphoreType.DMA((2,)),
        ],
        limit=44,
    )(sign, noisy_all, qkv_own, qkv_other, out_own, out_other)
    gap, gap_copies = local_call(
        gap_kernel, [VMEM], (array(SEQ, BLOCK), eight_kind), 1_000_000, 4_000_000
    )(exchange(gap_parts))
    gap_all = exchange(gap_copies)
    gap_crossed = swap(lax.dynamic_slice_in_dim(gap_all, (1 - group) * 4, 4, 0))
    grad_kinds = (grad_kind, array(BLOCK // 2, FF_LOCAL), array(BLOCK // 2, FF_LOCAL))
    down_grads = local_call(down_grad_kernel, [SMEM] + [VMEM] * 4, grad_kinds, matmul, 5_000_000)(
        at, gap_all, gap_crossed, hidden, hidden_crossed
    )
    down_shards = ring_scatter(*down_grads, at, "x", True)
    grad_down = narrow(direct_scatter(down_shards, "zh")).T

    here, away = local_call(
        slope_kernel, [SMEM] + [VMEM] * 4, (before_kind, before_kind), matmul, 6_000_000
    )(at, gap_all, gap_crossed, down_early, down_far)
    change = local_call(change_kernel, [VMEM] * 3, hidden_kind, 5_000_000, 2_800_000)(
        here, swap(away), before
    )
    up_grads = local_call(up_grad_kernel, [VMEM] * 4, grad_kinds, matmul, 5_000_000)(
        normed, normed_crossed, change, swap(change)
    )
    up_shards = ring_scatter(*up_grads, at, "x", False)
    grad_up = narrow(direct_scatter(up_shards, "zh"))
    return (latent[None], gap[None], grad_up, grad_down)


def solution(mesh):
    split = Mesh(
        mesh.devices.reshape(mesh.shape["group"], 4, 4, 4, 2), ("group", "x", "zh", "y", "zl")
    )
    in_specs = (
        P(SAMPLES),
        P(SAMPLES),
        P(SAMPLES, MODEL),
        P(MODEL, SAMPLES),
        P("group", None, None, MODEL),
        P("group", MODEL, None),
    )
    out_specs = (
        P(SAMPLES, None, MODEL),
        P(SAMPLES, None, MODEL),
        P(SAMPLES, MODEL),
        P(MODEL, SAMPLES),
    )
    return jax.shard_map(step, mesh=split, in_specs=in_specs, out_specs=out_specs, check_vma=False)
```

```python
import functools

import jax
import jax.numpy as jnp
from jax import lax
from jax.experimental import pallas as pl
from jax.experimental.pallas import tpu as pltpu
from jax.sharding import Mesh
from jax.sharding import PartitionSpec as P


D = 3072
FF_LOCAL = 768
HEAD_DIM = 128
SEQ = 256
STEPS = 1000
BATCH = 32
SHARD = 96
BLOCK = 384
SAMPLES = ("group", "x", "zh")
MODEL = ("y", "zl")

NORM_EPS = 1e-06
ROOT_THREE = 1.7320508
GELU_SCALE = 0.7978845608


def hop(value, axis, step):
    n = lax.axis_size(axis)
    return lax.ppermute(value, axis, [(i, (i + step) % n) for i in range(n)])


def wide(value):
    return value.astype(jnp.float32)


def narrow(value):
    return value.astype(jnp.bfloat16)


def direct_gather(block, axis, offsets=(1, 2, 3)):
    return [hop(block, axis, -k) for k in offsets]


def ring_gather(block, axis, ahead=None):
    half = block.shape[0] // 2
    left = hop(block, axis, 1)
    right = hop(block, axis, -1)
    top, bottom = left[:half], right[half:]
    if ahead is not None:
        top, bottom = jnp.concatenate([ahead[0], top]), jnp.concatenate([ahead[1], bottom])
    far_top = hop(top, axis, 1)
    far_bottom = hop(bottom, axis, -1)
    return [block, right, far_top, far_bottom, left]


def direct_scatter(parts, axis):
    return wide(parts[0]) + sum(wide(hop(parts[k], axis, k)) for k in (1, 3, 2))


def ring_scatter(grads, far_top, far_bottom, at, axis, turned):
    for_right = hop(far_top, axis, 1)
    for_left = hop(far_bottom, axis, -1)
    part = array(BLOCK, FF_LOCAL)
    right, left = local_call(merge_kernel, [VMEM] * 3, (part, part), 500_000, 3_000_000)(
        grads, for_right, for_left
    )
    from_left = hop(right, axis, 1)
    from_right = hop(left, axis, -1)
    return local_call(
        functools.partial(sum_kernel, turned=turned),
        [SMEM] + [VMEM] * 3,
        (array(SHARD, FF_LOCAL),) * 4,
        500_000,
        3_000_000,
    )(at, grads, from_left, from_right)


def exchange(parts):
    return lax.all_to_all(parts, MODEL, 0, 0, tiled=True)


def finish(mixing):
    mixing = mixing ^ mixing >> 15
    mixing = mixing * 1274126177
    mixing = mixing ^ mixing >> 13
    mixing = mixing * 1911520717
    mixing = mixing ^ mixing >> 16
    level = (mixing >> 7 & 65535).astype(jnp.float32)
    return ((level + 0.5) * (2.0 / 65536.0) - 1.0) * ROOT_THREE


def dot(left, right, left_dim=1, right_dim=0):
    return lax.dot_general(
        left, right, (((left_dim,), (right_dim,)), ((), ())), preferred_element_type=jnp.float32
    )


VMEM = pl.BlockSpec(memory_space=pltpu.VMEM)
SMEM = pl.BlockSpec(memory_space=pltpu.SMEM)
HBM = pl.BlockSpec(memory_space=pltpu.HBM)


def array(*shape, kind=jnp.bfloat16):
    return jax.ShapeDtypeStruct(shape, kind)


def local_call(kernel, ins, outs, flops, moved, scratch=(), limit=40, to=None):
    return pl.pallas_call(
        kernel,
        out_shape=outs,
        in_specs=ins,
        out_specs=to or jax.tree.map(lambda _: VMEM, outs),
        scratch_shapes=scratch,
        compiler_params=pltpu.CompilerParams(vmem_limit_bytes=limit << 20),
        cost_estimate=pl.CostEstimate(flops=flops, bytes_accessed=moved, transcendentals=0),
    )


def lane_chunk(c):
    return pl.ds(pl.multiple_of(c * 256, 256), 256)


def row_tile(i):
    return pl.ds(pl.multiple_of(i * 16, 16), 16)


def noise_kernel(seed_ref, feature_ref, own_ref, crossed_ref):
    start = seed_ref[0] * 747796405

    def tile(i, _):
        tokens = lax.broadcasted_iota(jnp.int32, (16, D), 0) + i * 16
        noise = finish(start + tokens * 1103515245 + feature_ref[...])
        scale = lax.rsqrt(jnp.mean(noise * noise, axis=-1, keepdims=True) + NORM_EPS)
        normed = narrow(noise * scale)
        own_ref[row_tile(i), :] = normed[:, : D // 2]
        crossed_ref[row_tile(i), :] = normed[:, D // 2 :]
        return 0

    lax.fori_loop(0, SEQ // 16, tile, 0)


def up_kernel(own_ref, crossed_ref, n0, n1, n3, r0, r1, far_top, far_bottom, r3, here, away):
    blocks = ((n0, r0), (n1, r1), (None, None), (n3, r3))

    def columns(c, _):
        lanes = lane_chunk(c)
        weights = [
            jnp.concatenate([near[:SHARD, lanes], rest[:, lanes]])
            if near is not None
            else jnp.concatenate([far_top[:, lanes], far_bottom[SHARD:, lanes]])
            for near, rest in blocks
        ]
        for normed, total in ((own_ref, here), (crossed_ref, away)):
            total[:, lanes] = sum(
                dot(normed[:, k * BLOCK : (k + 1) * BLOCK], block)
                for k, block in enumerate(weights)
            )
        return 0

    lax.fori_loop(0, FF_LOCAL // 256, columns, 0)


def hidden_kernel(here, arrived, before_ref, hidden_ref):
    def tile(i, _):
        rows = row_tile(i)
        value = here[rows, :] + arrived[rows, :]
        before_ref[rows, :] = value
        bend = jnp.tanh(GELU_SCALE * (value + 0.044715 * (value * value * value)))
        hidden_ref[rows, :] = narrow(0.5 * value * (1.0 + bend))
        return 0

    lax.fori_loop(0, SEQ // 16, tile, 0)


def merge_kernel(grads_ref, for_right, for_left, right_ref, left_ref):
    half = BLOCK // 2

    def tile(i, _):
        rows = row_tile(i)
        low = pl.ds(pl.multiple_of(half + i * 16, 16), 16)
        right_ref[rows, :] = narrow(wide(grads_ref[1, rows, :]) + wide(for_right[rows, :]))
        right_ref[low, :] = grads_ref[1, low, :]
        left_ref[rows, :] = grads_ref[3, rows, :]
        left_ref[low, :] = narrow(wide(grads_ref[3, low, :]) + wide(for_left[rows, :]))
        return 0

    lax.fori_loop(0, half // 16, tile, 0)


def sum_kernel(at_ref, grads_ref, from_left, from_right, *shards, turned):
    first = at_ref[2] if turned else 0
    for dz, shard in enumerate(shards):
        base = ((first + dz) & 3) * SHARD

        def tile(i, _):
            rows = pl.ds(pl.multiple_of(base + i * 16, 16), 16)
            shard[row_tile(i), :] = narrow(
                wide(grads_ref[0, rows, :]) + wide(from_left[rows, :]) + wide(from_right[rows, :])
            )
            return 0

        lax.fori_loop(0, SHARD // 16, tile, 0)


EARLY = (0, 1, 3)


def down_early_kernel(
    at_ref, hidden_ref, crossed_ref, n0, n1, n3, r0, r1, r3, down_ref, here_ref, away_ref
):
    for i, (near, rest) in enumerate(((n0, r0), (n1, r1), (n3, r3))):
        for dz in range(4):
            rows = pl.ds(pl.multiple_of(((at_ref[2] + dz) & 3) * SHARD, 32), SHARD)
            down_ref[i, rows, :] = (
                near[SHARD:, :] if dz == 0 else rest[(dz - 1) * SHARD : dz * SHARD, :]
            )

    def block(i, _):
        here_ref[i] = narrow(dot(hidden_ref[...], down_ref[i], 1, 1))
        away_ref[i] = narrow(dot(crossed_ref[...], down_ref[i], 1, 1))
        return 0

    lax.fori_loop(0, 3, block, 0)


def down_far_kernel(at_ref, crossed_ref, own_far, far_top, far_bottom, down_ref, away_ref):
    zh = at_ref[2]
    half = SHARD // 2
    for dz, pieces in enumerate(
        (
            (own_far[:half, :], own_far[half:SHARD, :]),
            (far_top[:half, :], far_top[half:SHARD, :]),
            (far_top[SHARD:, :], far_bottom[:half, :]),
            (far_bottom[half:SHARD, :], far_bottom[SHARD:, :]),
        )
    ):
        base = ((zh + dz) & 3) * SHARD
        for k, piece in enumerate(pieces):
            down_ref[pl.ds(pl.multiple_of(base + k * half, 16), half), :] = piece
    away_ref[...] = narrow(dot(crossed_ref[...], down_ref[...], 1, 1))


def parts_kernel(
    at_ref, hidden_hbm, down_ref, here_ref, arrived_ref, parts_ref, hidden_ref, sem
):
    load = pltpu.make_async_copy(hidden_hbm, hidden_ref, sem)
    load.start()
    group, x = at_ref[0], at_ref[1]
    for i, dx in enumerate(EARLY):
        parts_ref[group * 4 + ((x + dx) & 3)] = here_ref[i]
        parts_ref[(1 - group) * 4 + ((x + dx) & 3)] = arrived_ref[i]
    load.wait()
    parts_ref[group * 4 + ((x + 2) & 3)] = narrow(dot(hidden_ref[...], down_ref[...], 1, 1))


def score_kernel(
    sign_ref, noisy_ref, own_hbm, other_hbm, out_own_hbm, out_other_hbm, gap_ref,
    qkv_w, out_w, normed_ref, qkv_ref, mix_ref, qkv_sem, out_sem,
):
    loads = []
    for net, (source, out_source) in enumerate(
        ((own_hbm, out_own_hbm), (other_hbm, out_other_hbm))
    ):
        for k in range(3):
            loads.append(
                pltpu.make_async_copy(
                    source.at[k], qkv_w.at[net * 3 + k], qkv_sem.at[net * 3 + k]
                )
            )
        loads.append(pltpu.make_async_copy(out_source, out_w.at[net], out_sem.at[net]))
    for k in (0, 1, 2, 4, 5, 6, 3, 7):
        loads[k].start()

    def norm(i, _):
        rows = row_tile(i)
        blocks = [wide(noisy_ref[j, rows, :]) for j in range(8)]
        total = sum(jnp.sum(block * block, axis=-1, keepdims=True) for block in blocks)
        scale = lax.rsqrt(total * (1.0 / D) + NORM_EPS)
        for j in range(8):
            normed_ref[rows, j * BLOCK : (j + 1) * BLOCK] = narrow(blocks[j] * scale)
        return 0

    lax.fori_loop(0, SEQ // 16, norm, 0)

    def network(net, _):
        def project(k, _):
            slot = net * 3 + k
            pltpu.make_async_copy(own_hbm.at[0], qkv_w.at[slot], qkv_sem.at[slot]).wait()
            qkv_ref[k] = narrow(dot(normed_ref[...], qkv_w[slot]))
            return 0

        lax.fori_loop(0, 3, project, 0)
        sign = jnp.where(net == 0, sign_ref[0], -sign_ref[0])

        def attend(head, _):
            lanes = pl.ds(pl.multiple_of(head * HEAD_DIM, HEAD_DIM), HEAD_DIM)
            scores = dot(qkv_ref[0, :, lanes], qkv_ref[1, :, lanes], 1, 1) * HEAD_DIM ** (-0.5)
            expo = jnp.exp(scores)
            probs = narrow(expo / jnp.sum(expo, axis=-1, keepdims=True))
            attended = dot(probs, qkv_ref[2, :, lanes])
            mix_ref[net, :, lanes] = narrow(wide(narrow(attended)) * sign)
            return 0

        lax.fori_loop(0, BLOCK // HEAD_DIM, attend, 0)
        return 0

    lax.fori_loop(0, 2, network, 0)
    loads[3].wait()
    loads[7].wait()

    def emit(j, _):
        columns = pl.ds(pl.multiple_of(j * 2 * BLOCK, 2 * BLOCK), 2 * BLOCK)
        both = narrow(
            dot(mix_ref[0], out_w[0, :, columns]) + dot(mix_ref[1], out_w[1, :, columns])
        )
        gap_ref[2 * j] = both[:, :BLOCK]
        gap_ref[2 * j + 1] = both[:, BLOCK:]
        return 0

    lax.fori_loop(0, 4, emit, 0)


def slope_kernel(at_ref, gap_ref, crossed_ref, early_ref, far_ref, here, away):
    group, x = at_ref[0], at_ref[1]
    spots = [(x + dx) & 3 for dx in (*EARLY, 2)]

    def columns(c, _):
        lanes = lane_chunk(c)
        weights = [early_ref[i, :, lanes] for i in range(3)] + [far_ref[:, lanes]]
        here[:, lanes] = sum(dot(gap_ref[group * 4 + k], w) for k, w in zip(spots, weights))
        away[:, lanes] = sum(dot(crossed_ref[k], w) for k, w in zip(spots, weights))
        return 0

    lax.fori_loop(0, FF_LOCAL // 256, columns, 0)


def change_kernel(here, arrived, before_ref, change_ref):
    def tile(i, _):
        rows = row_tile(i)
        value = before_ref[rows, :]
        square = value * value
        bend = jnp.tanh(GELU_SCALE * (value + 0.044715 * square * value))
        turn = 0.5 * (1.0 + bend) + 0.5 * value * (1.0 - bend * bend) * GELU_SCALE * (
            1.0 + 3.0 * 0.044715 * square
        )
        change_ref[rows, :] = narrow((here[rows, :] + arrived[rows, :]) * turn)
        return 0

    lax.fori_loop(0, SEQ // 16, tile, 0)


def down_grad_kernel(at_ref, gap_ref, gap_crossed_ref, hidden_ref, hidden_crossed_ref, grad_ref, top, low):
    group, x = at_ref[0], at_ref[1]

    def block(k, _):
        spot = (x + k) & 3
        grad_ref[k] = narrow(
            (
                dot(gap_ref[group * 4 + spot], hidden_ref[...], 0, 0)
                + dot(gap_crossed_ref[spot], hidden_crossed_ref[...], 0, 0)
            )
            * (1.0 / BATCH)
        )
        return 0

    lax.fori_loop(0, 4, block, 0)
    top[...] = grad_ref[2, : BLOCK // 2]
    low[...] = grad_ref[2, BLOCK // 2 :]


def up_grad_kernel(own_ref, own_crossed_ref, change_ref, change_crossed_ref, grad_ref, top, low):
    def block(k, _):
        lanes = pl.ds(pl.multiple_of(k * BLOCK, BLOCK), BLOCK)
        grad_ref[k] = narrow(
            (
                dot(own_ref[:, lanes], change_ref[...], 0, 0)
                + dot(own_crossed_ref[:, lanes], change_crossed_ref[...], 0, 0)
            )
            * (1.0 / BATCH)
        )
        return 0

    lax.fori_loop(0, 4, block, 0)
    top[...] = grad_ref[2, : BLOCK // 2]
    low[...] = grad_ref[2, BLOCK // 2 :]


def latent_kernel(ids_ref, shift_ref, feature_ref, parts_ref, latent_ref, noisy_hbm, noisy_ref, sems):
    start = ids_ref[0] * 747796405
    shift = shift_ref[0]

    def tile(i, _):
        rows = row_tile(i)
        tokens = lax.broadcasted_iota(jnp.int32, (16, BLOCK), 0) + i * 16
        mixing = start + tokens * 1103515245 + feature_ref[...]
        mixed = sum(wide(parts_ref[j, rows, :]) for j in range(8))
        latent = narrow(finish(mixing) + mixed)
        latent_ref[rows, :] = latent
        noisy_ref[rows, :] = narrow(
            (1.0 - shift) * wide(latent) + shift * finish(mixing + 374761393)
        )
        return 0

    lax.fori_loop(0, SEQ // 16, tile, 0)
    spread(noisy_ref, noisy_hbm, sems)


def spread(block_ref, copies_hbm, sems):
    stores = [
        pltpu.make_async_copy(block_ref, copies_hbm.at[j], sems.at[j]) for j in range(8)
    ]
    for store in stores:
        store.start()
    for store in stores:
        store.wait()


def gap_kernel(parts_ref, gap_ref, copies_hbm, sems):
    def tile(i, _):
        rows = row_tile(i)
        gap = narrow(sum(wide(parts_ref[j, rows, :]) for j in range(8)))
        gap_ref[rows, :] = gap
        return 0

    lax.fori_loop(0, SEQ // 16, tile, 0)
    spread(gap_ref, copies_hbm, sems)


def swap(value):
    return hop(value, "group", 1)


def step(noise_seeds, timestep_ids, gen_up, gen_down, score_qkv, score_out):
    group, x, zh = (lax.axis_index(a) for a in SAMPLES)
    y, zl = (lax.axis_index(a) for a in MODEL)

    at = jnp.stack([group, x, zh])
    half_d = array(SEQ, D // 2)
    before_kind = array(SEQ, FF_LOCAL, kind=jnp.float32)
    hidden_kind = array(SEQ, FF_LOCAL)
    grad_kind = array(4, BLOCK, FF_LOCAL)
    matmul = 1_200_000_000

    down_shard = gen_down.T
    up_z = direct_gather(gen_up, "zh")
    both = jnp.concatenate([gen_up, down_shard])
    near_right, near_left = direct_gather(both, "x", (1, 3))
    near = [both, near_right, near_left]
    up_rest = ring_gather(jnp.concatenate(up_z), "x", (near_left[:SHARD], near_right[SHARD:]))
    down_z = direct_gather(down_shard, "zh")
    down_rest = ring_gather(jnp.concatenate(down_z), "x")
    qkv_own, out_own = score_qkv[0], score_out[0]
    qkv_other, out_other = swap(qkv_own), swap(out_own)

    index = lax.iota(jnp.int32, D)
    feature = (
        (((index // 1536) ^ group) * 4 + ((index // BLOCK + x) & 3)) * 4
        + ((index // SHARD + zh) & 3)
    ) * SHARD + index % SHARD
    normed, normed_away = local_call(
        noise_kernel, [SMEM, VMEM], (half_d, half_d), 30_000_000, 1_600_000
    )(noise_seeds, (feature * 668265263)[None])
    normed_crossed = swap(normed_away)
    here, away = local_call(
        up_kernel, [VMEM] * 10, (before_kind, before_kind), matmul, 5_000_000
    )(normed, normed_crossed, *near, *up_rest)
    before, hidden = local_call(
        hidden_kernel, [VMEM] * 2, (before_kind, hidden_kind), 3_000_000, 2_800_000
    )(here, swap(away))
    hidden_crossed = swap(hidden)
    three = array(3, SEQ, BLOCK)
    down_early, parts_here, parts_away = local_call(
        down_early_kernel,
        [SMEM] + [VMEM] * 8,
        (array(3, BLOCK, FF_LOCAL), three, three),
        900_000_000,
        6_000_000,
    )(
        at,
        hidden,
        hidden_crossed,
        *near,
        *(down_rest[k] for k in (0, 1, 4)),
    )
    eight_kind = array(8, SEQ, BLOCK)
    down_far, part_away = local_call(
        down_far_kernel,
        [SMEM] + [VMEM] * 4,
        (array(BLOCK, FF_LOCAL), array(SEQ, BLOCK)),
        150_000_000,
        2_000_000,
    )(at, hidden_crossed, up_rest[3], down_rest[2], down_rest[3])
    part_arrived = swap(part_away)
    parts = local_call(
        parts_kernel,
        [SMEM, HBM] + [VMEM] * 3,
        eight_kind,
        150_000_000,
        4_000_000,
        scratch=[pltpu.VMEM((SEQ, FF_LOCAL), jnp.bfloat16), pltpu.SemaphoreType.DMA],
    )(
        at,
        pltpu.with_memory_space_constraint(hidden, pltpu.HBM),
        down_far,
        parts_here,
        swap(parts_away),
    )
    parts = lax.dynamic_update_index_in_dim(
        parts, part_arrived, (1 - group) * 4 + ((x + 2) & 3), 0
    )

    local = lax.iota(jnp.int32, BLOCK) + (y * 2 + zl) * BLOCK
    shift = (timestep_ids[0].astype(jnp.float32) + 0.5) / STEPS
    latent, noisy = local_call(
        latent_kernel,
        [SMEM, SMEM, VMEM, VMEM],
        (array(SEQ, BLOCK), pltpu.HBM((8, SEQ, BLOCK), jnp.bfloat16)),
        9_000_000,
        4_000_000,
        scratch=[pltpu.VMEM((SEQ, BLOCK), jnp.bfloat16), pltpu.SemaphoreType.DMA((8,))],
        to=(VMEM, HBM),
        limit=16,
    )(noise_seeds, shift[None], (local * 668265263)[None], exchange(parts))
    noisy_all = exchange(noisy)
    sign = wide(2 * group - 1)[None]
    gap_parts = local_call(
        score_kernel,
        [SMEM, VMEM] + [HBM] * 4,
        array(8, SEQ, BLOCK),
        5_000_000_000,
        20_000_000,
        scratch=[
            pltpu.VMEM((6, D, BLOCK), jnp.bfloat16),
            pltpu.VMEM((2, BLOCK, D), jnp.bfloat16),
            pltpu.VMEM((SEQ, D), jnp.bfloat16),
            pltpu.VMEM((3, SEQ, BLOCK), jnp.bfloat16),
            pltpu.VMEM((2, SEQ, BLOCK), jnp.bfloat16),
            pltpu.SemaphoreType.DMA((6,)),
            pltpu.SemaphoreType.DMA((2,)),
        ],
        limit=44,
    )(
        sign,
        noisy_all,
        qkv_own,
        qkv_other,
        pltpu.with_memory_space_constraint(out_own, pltpu.HBM),
        out_other,
    )
    gap, gap_copies = local_call(
        gap_kernel,
        [VMEM],
        (array(SEQ, BLOCK), pltpu.HBM((8, SEQ, BLOCK), jnp.bfloat16)),
        1_000_000,
        4_000_000,
        scratch=[pltpu.SemaphoreType.DMA((8,))],
        to=(VMEM, HBM),
    )(exchange(gap_parts))
    gap_all = exchange(gap_copies)
    gap_crossed = swap(lax.dynamic_slice_in_dim(gap_all, (1 - group) * 4, 4, 0))
    grad_kinds = (grad_kind, array(BLOCK // 2, FF_LOCAL), array(BLOCK // 2, FF_LOCAL))
    down_grads = local_call(down_grad_kernel, [SMEM] + [VMEM] * 4, grad_kinds, matmul, 5_000_000)(
        at, gap_all, gap_crossed, hidden, hidden_crossed
    )
    down_shards = ring_scatter(*down_grads, at, "x", True)
    grad_down = narrow(direct_scatter(down_shards, "zh")).T

    here, away = local_call(
        slope_kernel, [SMEM] + [VMEM] * 4, (before_kind, before_kind), matmul, 6_000_000
    )(at, gap_all, gap_crossed, down_early, down_far)
    change = local_call(change_kernel, [VMEM] * 3, hidden_kind, 5_000_000, 2_800_000)(
        here, swap(away), before
    )
    up_grads = local_call(up_grad_kernel, [VMEM] * 4, grad_kinds, matmul, 5_000_000)(
        normed, normed_crossed, change, swap(change)
    )
    up_shards = ring_scatter(*up_grads, at, "x", False)
    grad_up = narrow(direct_scatter(up_shards, "zh"))
    return (latent[None], gap[None], grad_up, grad_down)


def solution(mesh):
    split = Mesh(
        mesh.devices.reshape(mesh.shape["group"], 4, 4, 4, 2), ("group", "x", "zh", "y", "zl")
    )
    in_specs = (
        P(SAMPLES),
        P(SAMPLES),
        P(SAMPLES, MODEL),
        P(MODEL, SAMPLES),
        P("group", None, None, MODEL),
        P("group", MODEL, None),
    )
    out_specs = (
        P(SAMPLES, None, MODEL),
        P(SAMPLES, None, MODEL),
        P(SAMPLES, MODEL),
        P(MODEL, SAMPLES),
    )
    return jax.shard_map(step, mesh=split, in_specs=in_specs, out_specs=out_specs, check_vma=False)
```

```python
import functools

import jax
import jax.numpy as jnp
from jax import lax
from jax.experimental import pallas as pl
from jax.experimental.pallas import tpu as pltpu
from jax.sharding import Mesh
from jax.sharding import PartitionSpec as P


D = 3072
FF_LOCAL = 768
HEAD_DIM = 128
SEQ = 256
STEPS = 1000
BATCH = 32
SHARD = 96
BLOCK = 384
SAMPLES = ("group", "x", "zh")
MODEL = ("y", "zl")

NORM_EPS = 1e-06
ROOT_THREE = 1.7320508
GELU_SCALE = 0.7978845608


def hop(value, axis, step):
    n = lax.axis_size(axis)
    return lax.ppermute(value, axis, [(i, (i + step) % n) for i in range(n)])


def wide(value):
    return value.astype(jnp.float32)


def narrow(value):
    return value.astype(jnp.bfloat16)


def direct_gather(block, axis, offsets=(1, 2, 3)):
    return [hop(block, axis, -k) for k in offsets]


def ring_gather(block, axis, ahead=None):
    half = block.shape[0] // 2
    left = hop(block, axis, 1)
    right = hop(block, axis, -1)
    top, bottom = left[:half], right[half:]
    if ahead is not None:
        top, bottom = jnp.concatenate([ahead[0], top]), jnp.concatenate([ahead[1], bottom])
    far_top = hop(top, axis, 1)
    far_bottom = hop(bottom, axis, -1)
    return [block, right, far_top, far_bottom, left]


def direct_scatter(parts, axis):
    return wide(parts[0]) + sum(wide(hop(parts[k], axis, k)) for k in (1, 3, 2))


def ring_scatter(grads, far_top, far_bottom, at, axis, turned):
    for_right = hop(far_top, axis, 1)
    for_left = hop(far_bottom, axis, -1)
    part = array(BLOCK, FF_LOCAL)
    right, left = local_call(merge_kernel, [VMEM] * 3, (part, part), 500_000, 3_000_000)(
        grads, for_right, for_left
    )
    from_left = hop(right, axis, 1)
    from_right = hop(left, axis, -1)
    return local_call(
        functools.partial(sum_kernel, turned=turned),
        [SMEM] + [VMEM] * 3,
        (array(SHARD, FF_LOCAL),) * 4,
        500_000,
        3_000_000,
    )(at, grads, from_left, from_right)


def exchange(parts):
    return lax.all_to_all(parts, MODEL, 0, 0, tiled=True)


def finish(mixing):
    mixing = mixing ^ mixing >> 15
    mixing = mixing * 1274126177
    mixing = mixing ^ mixing >> 13
    mixing = mixing * 1911520717
    mixing = mixing ^ mixing >> 16
    level = (mixing >> 7 & 65535).astype(jnp.float32)
    return ((level + 0.5) * (2.0 / 65536.0) - 1.0) * ROOT_THREE


def dot(left, right, left_dim=1, right_dim=0):
    return lax.dot_general(
        left, right, (((left_dim,), (right_dim,)), ((), ())), preferred_element_type=jnp.float32
    )


VMEM = pl.BlockSpec(memory_space=pltpu.VMEM)
SMEM = pl.BlockSpec(memory_space=pltpu.SMEM)
HBM = pl.BlockSpec(memory_space=pltpu.HBM)


def array(*shape, kind=jnp.bfloat16):
    return jax.ShapeDtypeStruct(shape, kind)


def local_call(kernel, ins, outs, flops, moved, scratch=(), limit=40, to=None):
    return pl.pallas_call(
        kernel,
        out_shape=outs,
        in_specs=ins,
        out_specs=to or jax.tree.map(lambda _: VMEM, outs),
        scratch_shapes=scratch,
        compiler_params=pltpu.CompilerParams(vmem_limit_bytes=limit << 20),
        cost_estimate=pl.CostEstimate(flops=flops, bytes_accessed=moved, transcendentals=0),
    )


def lane_chunk(c):
    return pl.ds(pl.multiple_of(c * 256, 256), 256)


def row_tile(i):
    return pl.ds(pl.multiple_of(i * 16, 16), 16)


def noise_kernel(seed_ref, feature_ref, own_ref, crossed_ref):
    start = seed_ref[0] * 747796405

    def tile(i, _):
        tokens = lax.broadcasted_iota(jnp.int32, (16, D), 0) + i * 16
        noise = finish(start + tokens * 1103515245 + feature_ref[...])
        scale = lax.rsqrt(jnp.mean(noise * noise, axis=-1, keepdims=True) + NORM_EPS)
        normed = narrow(noise * scale)
        own_ref[row_tile(i), :] = normed[:, : D // 2]
        crossed_ref[row_tile(i), :] = normed[:, D // 2 :]
        return 0

    lax.fori_loop(0, SEQ // 16, tile, 0)


def up_kernel(own_ref, crossed_ref, n0, n1, n3, r0, r1, far_top, far_bottom, r3, here, away):
    blocks = ((n0, r0), (n1, r1), (None, None), (n3, r3))

    def columns(c, _):
        lanes = lane_chunk(c)
        weights = [
            jnp.concatenate([near[:SHARD, lanes], rest[:, lanes]])
            if near is not None
            else jnp.concatenate([far_top[:, lanes], far_bottom[SHARD:, lanes]])
            for near, rest in blocks
        ]
        for normed, total in ((own_ref, here), (crossed_ref, away)):
            total[:, lanes] = sum(
                dot(normed[:, k * BLOCK : (k + 1) * BLOCK], block)
                for k, block in enumerate(weights)
            )
        return 0

    lax.fori_loop(0, FF_LOCAL // 256, columns, 0)


def hidden_kernel(here, arrived, before_ref, hidden_ref):
    def tile(i, _):
        rows = row_tile(i)
        value = here[rows, :] + arrived[rows, :]
        before_ref[rows, :] = value
        bend = jnp.tanh(GELU_SCALE * (value + 0.044715 * (value * value * value)))
        hidden_ref[rows, :] = narrow(0.5 * value * (1.0 + bend))
        return 0

    lax.fori_loop(0, SEQ // 16, tile, 0)


def merge_kernel(grads_ref, for_right, for_left, right_ref, left_ref):
    half = BLOCK // 2

    def tile(i, _):
        rows = row_tile(i)
        low = pl.ds(pl.multiple_of(half + i * 16, 16), 16)
        right_ref[rows, :] = narrow(wide(grads_ref[1, rows, :]) + wide(for_right[rows, :]))
        right_ref[low, :] = grads_ref[1, low, :]
        left_ref[rows, :] = grads_ref[3, rows, :]
        left_ref[low, :] = narrow(wide(grads_ref[3, low, :]) + wide(for_left[rows, :]))
        return 0

    lax.fori_loop(0, half // 16, tile, 0)


def sum_kernel(at_ref, grads_ref, from_left, from_right, *shards, turned):
    first = at_ref[2] if turned else 0
    for dz, shard in enumerate(shards):
        base = ((first + dz) & 3) * SHARD

        def tile(i, _):
            rows = pl.ds(pl.multiple_of(base + i * 16, 16), 16)
            shard[row_tile(i), :] = narrow(
                wide(grads_ref[0, rows, :]) + wide(from_left[rows, :]) + wide(from_right[rows, :])
            )
            return 0

        lax.fori_loop(0, SHARD // 16, tile, 0)


EARLY = (0, 1, 3)


def down_early_kernel(
    at_ref, hidden_ref, crossed_ref, n0, n1, n3, r0, r1, r3, down_ref, here_ref, away_ref
):
    for i, (near, rest) in enumerate(((n0, r0), (n1, r1), (n3, r3))):
        for dz in range(4):
            rows = pl.ds(pl.multiple_of(((at_ref[2] + dz) & 3) * SHARD, 32), SHARD)
            down_ref[i, rows, :] = (
                near[SHARD:, :] if dz == 0 else rest[(dz - 1) * SHARD : dz * SHARD, :]
            )

    def block(i, _):
        here_ref[i] = narrow(dot(hidden_ref[...], down_ref[i], 1, 1))
        away_ref[i] = narrow(dot(crossed_ref[...], down_ref[i], 1, 1))
        return 0

    lax.fori_loop(0, 3, block, 0)


def down_far_kernel(at_ref, crossed_ref, own_far, far_top, far_bottom, down_ref, away_ref):
    zh = at_ref[2]
    half = SHARD // 2
    for dz, pieces in enumerate(
        (
            (own_far[:half, :], own_far[half:SHARD, :]),
            (far_top[:half, :], far_top[half:SHARD, :]),
            (far_top[SHARD:, :], far_bottom[:half, :]),
            (far_bottom[half:SHARD, :], far_bottom[SHARD:, :]),
        )
    ):
        base = ((zh + dz) & 3) * SHARD
        for k, piece in enumerate(pieces):
            down_ref[pl.ds(pl.multiple_of(base + k * half, 16), half), :] = piece
    away_ref[...] = narrow(dot(crossed_ref[...], down_ref[...], 1, 1))


def parts_kernel(
    at_ref, hidden_hbm, down_ref, here_ref, arrived_ref, parts_ref, hidden_ref, sem
):
    load = pltpu.make_async_copy(hidden_hbm, hidden_ref, sem)
    load.start()
    group, x = at_ref[0], at_ref[1]
    for i, dx in enumerate(EARLY):
        parts_ref[group * 4 + ((x + dx) & 3)] = here_ref[i]
        parts_ref[(1 - group) * 4 + ((x + dx) & 3)] = arrived_ref[i]
    load.wait()
    parts_ref[group * 4 + ((x + 2) & 3)] = narrow(dot(hidden_ref[...], down_ref[...], 1, 1))


def score_kernel(
    sign_ref, noisy_ref, own_hbm, other_hbm, out_own_hbm, out_other_hbm, gap_ref,
    qkv_w, out_w, normed_ref, qkv_ref, mix_ref, qkv_sem, out_sem,
):
    loads = []
    for net, (source, out_source) in enumerate(
        ((own_hbm, out_own_hbm), (other_hbm, out_other_hbm))
    ):
        for k in range(3):
            loads.append(
                pltpu.make_async_copy(
                    source.at[k], qkv_w.at[net * 3 + k], qkv_sem.at[net * 3 + k]
                )
            )
        loads.append(pltpu.make_async_copy(out_source, out_w.at[net], out_sem.at[net]))
    for k in (0, 1, 2, 4, 5, 6, 3, 7):
        loads[k].start()

    def norm(i, _):
        rows = row_tile(i)
        blocks = [wide(noisy_ref[j, rows, :]) for j in range(8)]
        total = sum(jnp.sum(block * block, axis=-1, keepdims=True) for block in blocks)
        scale = lax.rsqrt(total * (1.0 / D) + NORM_EPS)
        for j in range(8):
            normed_ref[rows, j * BLOCK : (j + 1) * BLOCK] = narrow(blocks[j] * scale)
        return 0

    lax.fori_loop(0, SEQ // 16, norm, 0)

    def network(net, _):
        def project(k, _):
            slot = net * 3 + k
            pltpu.make_async_copy(own_hbm.at[0], qkv_w.at[slot], qkv_sem.at[slot]).wait()
            qkv_ref[k] = narrow(dot(normed_ref[...], qkv_w[slot]))
            return 0

        lax.fori_loop(0, 3, project, 0)
        sign = jnp.where(net == 0, sign_ref[0], -sign_ref[0])

        def attend(head, _):
            lanes = pl.ds(pl.multiple_of(head * HEAD_DIM, HEAD_DIM), HEAD_DIM)
            scores = dot(qkv_ref[0, :, lanes], qkv_ref[1, :, lanes], 1, 1) * HEAD_DIM ** (-0.5)
            expo = jnp.exp(scores)
            probs = narrow(expo / jnp.sum(expo, axis=-1, keepdims=True))
            attended = dot(probs, qkv_ref[2, :, lanes])
            mix_ref[net, :, lanes] = narrow(wide(narrow(attended)) * sign)
            return 0

        lax.fori_loop(0, BLOCK // HEAD_DIM, attend, 0)
        return 0

    lax.fori_loop(0, 2, network, 0)
    loads[3].wait()
    loads[7].wait()

    def emit(j, _):
        columns = pl.ds(pl.multiple_of(j * 2 * BLOCK, 2 * BLOCK), 2 * BLOCK)
        both = narrow(
            dot(mix_ref[0], out_w[0, :, columns]) + dot(mix_ref[1], out_w[1, :, columns])
        )
        gap_ref[2 * j] = both[:, :BLOCK]
        gap_ref[2 * j + 1] = both[:, BLOCK:]
        return 0

    lax.fori_loop(0, 4, emit, 0)


def slope_kernel(at_ref, gap_ref, crossed_ref, early_ref, far_ref, here, away):
    group, x = at_ref[0], at_ref[1]
    spots = [(x + dx) & 3 for dx in (*EARLY, 2)]

    def columns(c, _):
        lanes = lane_chunk(c)
        weights = [early_ref[i, :, lanes] for i in range(3)] + [far_ref[:, lanes]]
        here[:, lanes] = sum(dot(gap_ref[group * 4 + k], w) for k, w in zip(spots, weights))
        away[:, lanes] = sum(dot(crossed_ref[k], w) for k, w in zip(spots, weights))
        return 0

    lax.fori_loop(0, FF_LOCAL // 256, columns, 0)


def change_kernel(here, arrived, before_ref, change_ref):
    def tile(i, _):
        rows = row_tile(i)
        value = before_ref[rows, :]
        square = value * value
        bend = jnp.tanh(GELU_SCALE * (value + 0.044715 * square * value))
        turn = 0.5 * (1.0 + bend) + 0.5 * value * (1.0 - bend * bend) * GELU_SCALE * (
            1.0 + 3.0 * 0.044715 * square
        )
        change_ref[rows, :] = narrow((here[rows, :] + arrived[rows, :]) * turn)
        return 0

    lax.fori_loop(0, SEQ // 16, tile, 0)


def down_grad_kernel(at_ref, gap_ref, gap_crossed_ref, hidden_ref, hidden_crossed_ref, grad_ref, top, low):
    group, x = at_ref[0], at_ref[1]

    def block(k, _):
        spot = (x + k) & 3
        grad_ref[k] = narrow(
            (
                dot(gap_ref[group * 4 + spot], hidden_ref[...], 0, 0)
                + dot(gap_crossed_ref[spot], hidden_crossed_ref[...], 0, 0)
            )
            * (1.0 / BATCH)
        )
        return 0

    lax.fori_loop(0, 4, block, 0)
    top[...] = grad_ref[2, : BLOCK // 2]
    low[...] = grad_ref[2, BLOCK // 2 :]


def up_grad_kernel(own_ref, own_crossed_ref, change_ref, change_crossed_ref, grad_ref, top, low):
    def block(k, _):
        lanes = pl.ds(pl.multiple_of(k * BLOCK, BLOCK), BLOCK)
        grad_ref[k] = narrow(
            (
                dot(own_ref[:, lanes], change_ref[...], 0, 0)
                + dot(own_crossed_ref[:, lanes], change_crossed_ref[...], 0, 0)
            )
            * (1.0 / BATCH)
        )
        return 0

    lax.fori_loop(0, 4, block, 0)
    top[...] = grad_ref[2, : BLOCK // 2]
    low[...] = grad_ref[2, BLOCK // 2 :]


def latent_kernel(ids_ref, shift_ref, feature_ref, parts_ref, latent_ref, noisy_hbm, noisy_ref, sems):
    start = ids_ref[0] * 747796405
    shift = shift_ref[0]

    def tile(i, _):
        rows = row_tile(i)
        tokens = lax.broadcasted_iota(jnp.int32, (16, BLOCK), 0) + i * 16
        mixing = start + tokens * 1103515245 + feature_ref[...]
        mixed = sum(wide(parts_ref[j, rows, :]) for j in range(8))
        latent = narrow(finish(mixing) + mixed)
        latent_ref[rows, :] = latent
        noisy_ref[rows, :] = narrow(
            (1.0 - shift) * wide(latent) + shift * finish(mixing + 374761393)
        )
        return 0

    spread(tile, noisy_ref, noisy_hbm, sems)


def spread(tile, block_ref, copies_hbm, sems):
    stores = []
    for quarter in range(4):
        lax.fori_loop(quarter * 4, quarter * 4 + 4, tile, 0)
        rows = pl.ds(quarter * (SEQ // 4), SEQ // 4)
        for j in range(8):
            stores.append(
                pltpu.make_async_copy(
                    block_ref.at[rows, :], copies_hbm.at[j, rows, :], sems.at[quarter, j]
                )
            )
            stores[-1].start()
    for store in stores:
        store.wait()


def gap_kernel(parts_ref, gap_ref, copies_hbm, sems):
    def tile(i, _):
        rows = row_tile(i)
        gap = narrow(sum(wide(parts_ref[j, rows, :]) for j in range(8)))
        gap_ref[rows, :] = gap
        return 0

    spread(tile, gap_ref, copies_hbm, sems)


def swap(value):
    return hop(value, "group", 1)


def step(noise_seeds, timestep_ids, gen_up, gen_down, score_qkv, score_out):
    group, x, zh = (lax.axis_index(a) for a in SAMPLES)
    y, zl = (lax.axis_index(a) for a in MODEL)

    at = jnp.stack([group, x, zh])
    half_d = array(SEQ, D // 2)
    before_kind = array(SEQ, FF_LOCAL, kind=jnp.float32)
    hidden_kind = array(SEQ, FF_LOCAL)
    grad_kind = array(4, BLOCK, FF_LOCAL)
    matmul = 1_200_000_000

    down_shard = gen_down.T
    up_z = direct_gather(gen_up, "zh")
    both = jnp.concatenate([gen_up, down_shard])
    near_right, near_left = direct_gather(both, "x", (1, 3))
    near = [both, near_right, near_left]
    up_rest = ring_gather(jnp.concatenate(up_z), "x", (near_left[:SHARD], near_right[SHARD:]))
    down_z = direct_gather(down_shard, "zh")
    down_rest = ring_gather(jnp.concatenate(down_z), "x")
    qkv_own, out_own = score_qkv[0], score_out[0]
    qkv_other, out_other = swap(qkv_own), swap(out_own)

    index = lax.iota(jnp.int32, D)
    feature = (
        (((index // 1536) ^ group) * 4 + ((index // BLOCK + x) & 3)) * 4
        + ((index // SHARD + zh) & 3)
    ) * SHARD + index % SHARD
    normed, normed_away = local_call(
        noise_kernel, [SMEM, VMEM], (half_d, half_d), 30_000_000, 1_600_000
    )(noise_seeds, (feature * 668265263)[None])
    normed_crossed = swap(normed_away)
    here, away = local_call(
        up_kernel, [VMEM] * 10, (before_kind, before_kind), matmul, 5_000_000
    )(normed, normed_crossed, *near, *up_rest)
    before, hidden = local_call(
        hidden_kernel, [VMEM] * 2, (before_kind, hidden_kind), 3_000_000, 2_800_000
    )(here, swap(away))
    hidden_crossed = swap(hidden)
    three = array(3, SEQ, BLOCK)
    down_early, parts_here, parts_away = local_call(
        down_early_kernel,
        [SMEM] + [VMEM] * 8,
        (array(3, BLOCK, FF_LOCAL), three, three),
        900_000_000,
        6_000_000,
    )(
        at,
        hidden,
        hidden_crossed,
        *near,
        *(down_rest[k] for k in (0, 1, 4)),
    )
    eight_kind = array(8, SEQ, BLOCK)
    down_far, part_away = local_call(
        down_far_kernel,
        [SMEM] + [VMEM] * 4,
        (array(BLOCK, FF_LOCAL), array(SEQ, BLOCK)),
        150_000_000,
        2_000_000,
    )(at, hidden_crossed, up_rest[3], down_rest[2], down_rest[3])
    part_arrived = swap(part_away)
    parts = local_call(
        parts_kernel,
        [SMEM, HBM] + [VMEM] * 3,
        eight_kind,
        150_000_000,
        4_000_000,
        scratch=[pltpu.VMEM((SEQ, FF_LOCAL), jnp.bfloat16), pltpu.SemaphoreType.DMA],
    )(
        at,
        pltpu.with_memory_space_constraint(hidden, pltpu.HBM),
        down_far,
        parts_here,
        swap(parts_away),
    )
    parts = lax.dynamic_update_index_in_dim(
        parts, part_arrived, (1 - group) * 4 + ((x + 2) & 3), 0
    )

    local = lax.iota(jnp.int32, BLOCK) + (y * 2 + zl) * BLOCK
    shift = (timestep_ids[0].astype(jnp.float32) + 0.5) / STEPS
    latent, noisy = local_call(
        latent_kernel,
        [SMEM, SMEM, VMEM, VMEM],
        (array(SEQ, BLOCK), pltpu.HBM((8, SEQ, BLOCK), jnp.bfloat16)),
        9_000_000,
        4_000_000,
        scratch=[pltpu.VMEM((SEQ, BLOCK), jnp.bfloat16), pltpu.SemaphoreType.DMA((4, 8))],
        to=(VMEM, HBM),
        limit=16,
    )(noise_seeds, shift[None], (local * 668265263)[None], exchange(parts))
    noisy_all = exchange(noisy)
    sign = wide(2 * group - 1)[None]
    gap_parts = local_call(
        score_kernel,
        [SMEM, VMEM] + [HBM] * 4,
        array(8, SEQ, BLOCK),
        5_000_000_000,
        20_000_000,
        scratch=[
            pltpu.VMEM((6, D, BLOCK), jnp.bfloat16),
            pltpu.VMEM((2, BLOCK, D), jnp.bfloat16),
            pltpu.VMEM((SEQ, D), jnp.bfloat16),
            pltpu.VMEM((3, SEQ, BLOCK), jnp.bfloat16),
            pltpu.VMEM((2, SEQ, BLOCK), jnp.bfloat16),
            pltpu.SemaphoreType.DMA((6,)),
            pltpu.SemaphoreType.DMA((2,)),
        ],
        limit=44,
    )(
        sign,
        noisy_all,
        qkv_own,
        qkv_other,
        pltpu.with_memory_space_constraint(out_own, pltpu.HBM),
        out_other,
    )
    gap, gap_copies = local_call(
        gap_kernel,
        [VMEM],
        (array(SEQ, BLOCK), pltpu.HBM((8, SEQ, BLOCK), jnp.bfloat16)),
        1_000_000,
        4_000_000,
        scratch=[pltpu.SemaphoreType.DMA((4, 8))],
        to=(VMEM, HBM),
    )(exchange(gap_parts))
    gap_all = exchange(gap_copies)
    gap_crossed = swap(lax.dynamic_slice_in_dim(gap_all, (1 - group) * 4, 4, 0))
    grad_kinds = (grad_kind, array(BLOCK // 2, FF_LOCAL), array(BLOCK // 2, FF_LOCAL))
    down_grads = local_call(down_grad_kernel, [SMEM] + [VMEM] * 4, grad_kinds, matmul, 5_000_000)(
        at, gap_all, gap_crossed, hidden, hidden_crossed
    )
    down_shards = ring_scatter(*down_grads, at, "x", True)
    grad_down = narrow(direct_scatter(down_shards, "zh")).T

    here, away = local_call(
        slope_kernel, [SMEM] + [VMEM] * 4, (before_kind, before_kind), matmul, 6_000_000
    )(at, gap_all, gap_crossed, down_early, down_far)
    change = local_call(change_kernel, [VMEM] * 3, hidden_kind, 5_000_000, 2_800_000)(
        here, swap(away), before
    )
    up_grads = local_call(up_grad_kernel, [VMEM] * 4, grad_kinds, matmul, 5_000_000)(
        normed, normed_crossed, change, swap(change)
    )
    up_shards = ring_scatter(*up_grads, at, "x", False)
    grad_up = narrow(direct_scatter(up_shards, "zh"))
    return (latent[None], gap[None], grad_up, grad_down)


def solution(mesh):
    split = Mesh(
        mesh.devices.reshape(mesh.shape["group"], 4, 4, 4, 2), ("group", "x", "zh", "y", "zl")
    )
    in_specs = (
        P(SAMPLES),
        P(SAMPLES),
        P(SAMPLES, MODEL),
        P(MODEL, SAMPLES),
        P("group", None, None, MODEL),
        P("group", MODEL, None),
    )
    out_specs = (
        P(SAMPLES, None, MODEL),
        P(SAMPLES, None, MODEL),
        P(SAMPLES, MODEL),
        P(MODEL, SAMPLES),
    )
    return jax.shard_map(step, mesh=split, in_specs=in_specs, out_specs=out_specs, check_vma=False)
```
